128 devices in a mesh: shard: 16 (over y, z), tensor: 8 (over x, core).
Axes of the slice: x: 4, y: 4, z: 4, core: 2. Of those that a mesh axis runs over, the one named last changes fastest.
Arguments:
- grads: bfloat16 [32, 896, 16640], P('shard', None, 'tensor'), may hold values from -1 to 1
- small_grads: bfloat16 [32, 2944], P('shard', 'tensor'), may hold values from -6 to 6
- counts: int32 [16], P('shard'), may hold values from 1 to 2
- step: int32 [1], replicated, may hold values from 1 to 1000
- master: float32 [896, 16640], P(('shard', 'tensor')), may hold values from -0.01953125 to 0.01953125
- moment_one: float32 [896, 16640], P(('shard', 'tensor')), may hold values from -7.6293945e-05 to 7.6293945e-05
- moment_two: float32 [896, 16640], P(('shard', 'tensor')), may hold values from 1e-12 to 1e-09
- average: float32 [896, 16640], P(('shard', 'tensor')), may hold values from -0.01953125 to 0.01953125
- small_master: float32 [8, 368], P('tensor', 'shard'), may hold values from -0.046875 to 0.046875
- small_one: float32 [8, 368], P('tensor', 'shard'), may hold values from -0.0078125 to 0.0078125
- small_two: float32 [8, 368], P('tensor', 'shard'), may hold values from 1e-09 to 1e-07
- small_average: float32 [8, 368], P('tensor', 'shard'), may hold values from -0.046875 to 0.046875
Outputs:
- new_master: float32 [896, 16640], P(('shard', 'tensor'))
- new_one: float32 [896, 16640], P(('shard', 'tensor'))
- new_two: float32 [896, 16640], P(('shard', 'tensor'))
- small_new: float32 [8, 368], P('tensor', 'shard')
- small_new_one: float32 [8, 368], P('tensor', 'shard')
- small_new_two: float32 [8, 368], P('tensor', 'shard')
- weights_out: bfloat16 [896, 16640], P(None, 'tensor')
- small_weights_out: bfloat16 [2944], P('tensor')
- average_out: float32 [896, 16640], P(None, 'tensor')
- small_average_out: float32 [2944], P('tensor')
The draws below stay inside these ranges and needn't reach their ends.
All inputs are finite; a program needn't handle non-finite values.
Results may differ from the reference program's by a relative error of at most 0.001.
Values may be sent and summed in bfloat16 or wider, within the bound.
A program may use at most 256 MiB of HBM per device.

```python
import math
import jax
import jax.numpy as jnp
from jax import lax

D = 896
MB_DEV = 2
COLS = 16640
SMALL = 2944
N_SHARD = 16
N_TENSOR = 8


def draw_grads(key, part):
    key_rows = jax.random.fold_in(key, 0)
    key_cols = jax.random.fold_in(key, 1)
    key_base = jax.random.fold_in(key, 2)
    key_shard = jax.random.fold_in(key, 4)
    rows = jnp.exp(jax.random.uniform(key_rows, (1, 1, D, 1), jnp.float32, 0.0, math.log(10.0)))
    cols = jnp.exp(jax.random.uniform(key_cols, (1, 1, 1, COLS), jnp.float32, 0.0, math.log(10.0)))
    shard_part = 1.5 * jax.random.normal(key_shard, (N_SHARD, 1, D, COLS), jnp.float32)
    base = jax.random.normal(key_base, (N_SHARD, MB_DEV, D, COLS), jnp.float32)
    values = (base + shard_part) * rows * cols * 0.0005
    values = values.reshape(N_SHARD * MB_DEV, D, COLS)
    return jnp.clip(values, -1.0, 1.0).astype(jnp.bfloat16)


def set_ends(array, own_key, least, largest):
    longest = array.shape.index(max(array.shape))
    spots = []
    for shift in (0, 1):
        where = [jax.random.randint(jax.random.fold_in(own_key, axis), (), 0, length) for axis, length in enumerate(array.shape)]
        where[longest] = (where[longest] + shift) % array.shape[longest]
        spots.append(tuple(where))
    return array.at[spots[0]].set(least).at[spots[1]].set(largest)


def shard_levels(key, shape, cuts, smallest, high):
    level, own = 1.0, jax.random.fold_in(key, 6)
    for position, shards_of in cuts:
        heights = jnp.exp(jax.random.uniform(jax.random.fold_in(own, position), (shards_of,), jnp.float32, smallest / len(cuts), high / len(cuts)))
        level = level * jnp.repeat(heights, shape[position] // shards_of).reshape([-1 if axis == position else 1 for axis in range(len(shape))])
    return level


def bell_draw(own_key, shape, scale, most, cuts=(), held_as=jnp.bfloat16):
    entries = scale * jax.random.normal(own_key, shape, jnp.float32)
    if cuts:
        entries = entries * shard_levels(own_key, shape, cuts, -0.22, 0.18)
    return jnp.clip(entries, -most, most).astype(held_as)


def setup_inputs(seed: int = 0) -> dict:
    seeds = jax.random.split(jax.random.key(seed), 13)
    grads = draw_grads(jax.random.fold_in(seeds[12], 71), 0)
    small_grads = bell_draw(seeds[1], (N_SHARD * MB_DEV, SMALL), 1.0, 6.0, ((0, 16), (1, 8)))
    counts = set_ends(jax.random.randint(seeds[2], (N_SHARD,), 1, MB_DEV + 1), jax.random.fold_in(seeds[2], 1), 1, MB_DEV).astype(jnp.int32)
    step = jax.random.randint(seeds[3], (1,), 1, 1001).astype(jnp.int32)
    master = bell_draw(seeds[4], (D, COLS), (100 * D) ** -0.5, 0.01953125, ((0, 128),), jnp.float32)
    moment_one = bell_draw(seeds[5], (D, COLS), 0.000005, 7.62939453125e-05, ((0, 128),), jnp.float32)
    moment_two = jnp.clip(jnp.exp(math.log(9.999999717180685e-10) - 6.9077553 * jax.random.uniform(seeds[6], (D, COLS), jnp.float32) ** shard_levels(seeds[6], (D, COLS), ((0, 128),), -0.2, 0.2)), 9.999999960041972e-13, 9.999999717180685e-10)
    average = bell_draw(seeds[7], (D, COLS), (100 * D) ** -0.5, 0.01953125, ((0, 128),), jnp.float32)
    small_master = bell_draw(seeds[8], (N_TENSOR, SMALL // N_TENSOR), 0.003, 0.046875, ((0, 8), (1, 16)), jnp.float32)
    small_one = bell_draw(seeds[9], (N_TENSOR, SMALL // N_TENSOR), 0.0005, 0.0078125, ((0, 8), (1, 16)), jnp.float32)
    small_two = jnp.clip(jnp.exp(math.log(1.0000000116860974e-07) - 4.6051702 * jax.random.uniform(seeds[10], (N_TENSOR, SMALL // N_TENSOR), jnp.float32) ** shard_levels(seeds[10], (N_TENSOR, SMALL // N_TENSOR), ((0, 8), (1, 16)), -0.2, 0.2)), 9.999999717180685e-10, 1.0000000116860974e-07)
    small_average = bell_draw(seeds[11], (N_TENSOR, SMALL // N_TENSOR), 0.003, 0.046875, ((0, 8), (1, 16)), jnp.float32)
    return {"grads": grads, "small_grads": small_grads, "counts": counts, "step": step, "master": master, "moment_one": moment_one, "moment_two": moment_two, "average": average, "small_master": small_master, "small_one": small_one, "small_two": small_two, "small_average": small_average}


learn_rate = 0.002
beta_one = 0.9
beta_two = 0.999
adam_eps = 1e-08
weight_decay = 0.1
clip_norm = 1.0
decay_rate = 0.99

def adam_update(param, first, second, gradient, time, decay):
    first_new = beta_one * first + (1.0 - beta_one) * gradient
    second_new = beta_two * second + (1.0 - beta_two) * gradient * gradient
    bias_one = 1.0 - jnp.power(jnp.float32(beta_one), time)
    bias_two = 1.0 - jnp.power(jnp.float32(beta_two), time)
    ratio = first_new / bias_one / (jnp.sqrt(second_new / bias_two) + adam_eps)
    param_new = param - learn_rate * (ratio + decay * param)
    return (param_new, first_new, second_new)

def reference(grads, small_grads, counts, step, master, moment_one, moment_two, average, small_master, small_one, small_two, small_average):
    micro = grads.shape[0] // counts.shape[0]
    valid = (jnp.arange(micro, dtype=jnp.int32)[None, :] < counts[:, None]).astype(jnp.float32).reshape(-1)

    def accumulate(carry, index):
        return (carry + valid[index] * grads[index].astype(jnp.float32), None)
    big_sum, _ = lax.scan(accumulate, jnp.zeros(grads.shape[1:], jnp.float32), jnp.arange(grads.shape[0], dtype=jnp.int32))
    small_sum = lax.optimization_barrier(jnp.sum(valid[:, None] * small_grads.astype(jnp.float32), axis=0)).reshape(small_master.shape)
    norm = jnp.sqrt(jnp.sum(big_sum * big_sum) + jnp.sum(small_sum * small_sum))
    factor = jnp.minimum(1.0, clip_norm / (norm + 1e-06))
    time = step[0].astype(jnp.float32)
    new_master, new_one, new_two = adam_update(master, moment_one, moment_two, big_sum * factor, time, weight_decay)
    small_new, small_new_one, small_new_two = adam_update(small_master, small_one, small_two, small_sum * factor, time, 0.0)
    average_out = decay_rate * average + (1.0 - decay_rate) * new_master
    small_average_out = (decay_rate * small_average + (1.0 - decay_rate) * small_new).reshape(-1)
    weights_out = new_master.astype(jnp.bfloat16)
    small_weights_out = small_new.reshape(-1).astype(jnp.bfloat16)
    return (new_master, new_one, new_two, small_new, small_new_one, small_new_two, weights_out, small_weights_out, average_out, small_average_out)
```

```python
import jax
import jax.numpy as jnp
from jax import lax
from jax.experimental import pallas as pl
from jax.experimental.pallas import tpu as pltpu
from jax.sharding import PartitionSpec as P

learn_rate = 0.002
beta_one = 0.9
beta_two = 0.999
adam_eps = 1e-08
weight_decay = 0.1
clip_norm = 1.0
decay_rate = 0.99

MESH = pl.DeviceIdType.MESH
RING = 4
SHARDS = RING * RING
TENSORS = 8
ROWS = 56
MINE = 7
COLS = 2080
ALL_COLS = COLS * TENSORS
SMALL = 368
SEG = 23
LANES = 384
PARTS = ((0, 512), (512, 512), (1024, 512), (1536, 544))
TOP = 32700.0
SUM_MAX = 2.0
AVERAGE_MAX = 0.03


def encode(x, most):
    scaled = jnp.abs(x) * (TOP**4 / most) + 1e-20
    root = (lax.rsqrt(lax.rsqrt(scaled)) + 0.5).astype(jnp.int32)
    return jnp.where(x < 0.0, -root, root).astype(jnp.int16)


def decode(code, most):
    root = code.astype(jnp.int32).astype(jnp.float32)
    return (root * root) * (root * jnp.abs(root)) * (most / TOP**4)


def adam(param, first, second, gradient, bias_one, bias_two, decay):
    first_new = beta_one * first + (1.0 - beta_one) * gradient
    second_new = beta_two * second + (1.0 - beta_two) * gradient * gradient
    ratio = first_new / bias_one / (jnp.sqrt(second_new / bias_two) + adam_eps)
    return param - learn_rate * (ratio + decay * param), first_new, second_new


def wrap(position, shift, size):
    return lax.rem(position + (shift + size), size)


def step_kernel(
    scal,
    small_in,
    grads_hbm,
    master_hbm,
    one_hbm,
    two_hbm,
    average_hbm,
    master_out,
    one_out,
    two_out,
    small_out,
    weights_out,
    codes_out,
    gv,
    pm,
    p1,
    p2,
    pa,
    om,
    o1,
    o2,
    big_send,
    big_recv,
    kept,
    mid_send,
    mid_recv,
    total,
    chunk_send,
    chunk_recv,
    wchunk_send,
    wchunk_recv,
    achunk_send,
    achunk_recv,
    norm_send,
    norm_t,
    norm_y,
    norm_z,
    small_send,
    small_y,
    small_z,
    wall,
    aall,
    load_sem,
    store_sem,
    rs_send_sem,
    rs_recv_sem,
    t_send_sem,
    t_recv_sem,
    r_send_sem,
    r_recv_sem,
    ag_send_sem,
    ag_recv_sem,
):
    s = lax.axis_index("shard")
    t = lax.axis_index("tensor")
    pos = (lax.div(s, RING), lax.rem(s, RING))
    core_sign = 1 - 2 * lax.rem(t, 2)

    def ring_device(axis, p):
        return (p * RING + pos[1], t) if axis == 0 else (pos[0] * RING + p, t)

    def shard_of(axis, p, k):
        return p * RING + k if axis == 0 else k * RING + p

    loads = []
    for i, (src, dst) in enumerate(
        ((grads_hbm, gv), (master_hbm, pm), (one_hbm, p1), (two_hbm, p2), (average_hbm, pa))
    ):
        load = pltpu.make_async_copy(src, dst, load_sem.at[i])
        load.start()
        loads.append(load)

    barrier = pltpu.get_barrier_semaphore()
    for axis in range(2):
        for d in range(1, RING):
            pl.semaphore_signal(
                barrier, inc=1, device_id=ring_device(axis, wrap(pos[axis], d, RING)), device_id_type=MESH
            )
    for d in range(1, TENSORS):
        pl.semaphore_signal(barrier, inc=1, device_id=(s, wrap(t, d, TENSORS)), device_id_type=MESH)
    pl.semaphore_wait(barrier, 2 * (RING - 1) + TENSORS - 1)

    pending = []

    def send(src, dst, send_sem, recv_sem, device):
        copy = pltpu.make_async_remote_copy(
            src_ref=src, dst_ref=dst, send_sem=send_sem, recv_sem=recv_sem, device_id=device, device_id_type=MESH
        )
        copy.start()
        pending.append(copy)
        return copy

    def ring_share(kind, axis, src, dst):
        return [
            send(
                src,
                dst.at[d - 1],
                r_send_sem.at[kind, d - 1],
                r_recv_sem.at[kind, d - 1],
                ring_device(axis, wrap(pos[axis], d, RING)),
            )
            for d in range(1, RING)
        ]

    small_copies = ring_share(0, 0, small_in, small_y)
    loads[0].wait()
    valid_one, valid_two = scal[0], scal[1]

    def local(shard, q):
        first, width = PARTS[q]
        a = gv[0, shard, :, pl.ds(first, width)].astype(jnp.float32)
        b = gv[1, shard, :, pl.ds(first, width)].astype(jnp.float32)
        return valid_one * a + valid_two * b

    axes = ((0, 1), (0, 1), (1, 0), (1, 0))
    signs = (core_sign, -core_sign, core_sign, -core_sign)
    order = [[wrap(pos[axes[q][1]], k, RING) for k in (2, signs[q], -signs[q], 0)] for q in range(4)]
    early = [[None] * 2 for _ in range(4)]
    for slot in range(2):
        for q in range(4):
            axis, sign = axes[q][0], signs[q]
            p = pos[axis]
            dest = wrap(p, 2, RING) if slot == 0 else wrap(p, sign, RING)

            def fill(k, carry, q=q, axis=axis, dest=dest, slot=slot):
                big_send[q][slot, k] = encode(local(shard_of(axis, dest, k), q), SUM_MAX)
                return carry

            lax.fori_loop(0, RING, fill, 0)
            to = wrap(p, -sign, RING) if slot == 0 else dest
            early[q][slot] = send(
                big_send[q].at[slot],
                big_recv[q].at[slot],
                rs_send_sem.at[q, slot],
                rs_recv_sem.at[q, slot],
                ring_device(axis, to),
            )
    relayed = [[None] * RING for _ in range(4)]
    for q in range(4):
        early[q][0].wait_recv()
    for i in range(RING):
        for q in range(4):
            axis, sign = axes[q][0], signs[q]
            dest = wrap(pos[axis], -sign, RING)
            k = order[q][i]
            came = decode(big_recv[q][0, k], SUM_MAX)
            big_send[q][2, k] = encode(local(shard_of(axis, dest, k), q) + came, 2 * SUM_MAX)
            relayed[q][i] = send(
                big_send[q].at[2, k],
                big_recv[q].at[2, k],
                rs_send_sem.at[q, 2 + i],
                rs_recv_sem.at[q, 2 + i],
                ring_device(axis, dest),
            )
    for copy in small_copies:
        copy.wait_recv()
    small_send[...] = small_in[...] + small_y[0] + small_y[1] + small_y[2]
    small_copies = ring_share(1, 1, small_send, small_z)
    for q in range(4):
        early[q][1].wait_recv()

    later = [[None] * 3 for _ in range(4)]
    for i in range(RING):
        for q in range(4):
            (axis, other), sign = axes[q], signs[q]
            k = order[q][i]
            relayed[q][i].wait_recv()
            piece = (
                local(shard_of(axis, pos[axis], k), q)
                + decode(big_recv[q][1, k], SUM_MAX)
                + decode(big_recv[q][2, k], 2 * SUM_MAX)
            )
            if i >= 2:
                kept[q][i - 2] = piece
                continue
            mid_send[q][i] = encode(piece, 4 * SUM_MAX)
            to = wrap(pos[other], -sign if i == 0 else sign, RING)
            later[q][i] = send(
                mid_send[q].at[i],
                mid_recv[q].at[i],
                rs_send_sem.at[q, 6 + i],
                rs_recv_sem.at[q, 6 + i],
                ring_device(other, to),
            )
    for q in range(4):
        other, sign = axes[q][1], signs[q]
        later[q][0].wait_recv()
        mid_send[q][2] = encode(kept[q][0] + decode(mid_recv[q][0], 4 * SUM_MAX), 8 * SUM_MAX)
        later[q][2] = send(
            mid_send[q].at[2],
            mid_recv[q].at[2],
            rs_send_sem.at[q, 8],
            rs_recv_sem.at[q, 8],
            ring_device(other, wrap(pos[other], -sign, RING)),
        )
    for copy in small_copies:
        copy.wait_recv()
    small_all = small_send[...] + small_z[0] + small_z[1] + small_z[2]
    small_sum = small_all[0:1]
    squares = jnp.sum(small_sum * small_sum) * (1.0 / SHARDS)
    for q in range(4):
        first, width = PARTS[q]
        later[q][1].wait_recv()
        later[q][2].wait_recv()
        piece = kept[q][1] + decode(mid_recv[q][1], 4 * SUM_MAX) + decode(mid_recv[q][2], 8 * SUM_MAX)
        total[:, pl.ds(first, width)] = piece
        squares = squares + jnp.sum(piece * piece)

    norm_send[0] = jnp.full((8, 128), squares, jnp.float32)
    norm_copies = []
    for d in range(1, TENSORS):
        norm_copies.append(
            send(
                norm_send.at[0],
                norm_t.at[d - 1],
                t_send_sem.at[0, d],
                t_recv_sem.at[0, d],
                (s, wrap(t, d, TENSORS)),
            )
        )
    for j in range(TENSORS):
        chunk_send[j] = encode(total[pl.ds(MINE * j, MINE), :], 16 * SUM_MAX)
    chunk_recv[t] = chunk_send[t]

    def exchange(kind, src, dst):
        copies = []
        for d in range(1, TENSORS):
            to = wrap(t, d, TENSORS)
            copies.append(
                send(src.at[to], dst.at[t], t_send_sem.at[kind, d], t_recv_sem.at[kind, d], (s, to))
            )
        return copies

    chunk_copies = exchange(1, chunk_send, chunk_recv)
    for copy in norm_copies:
        copy.wait_recv()
    norm = norm_send[0]
    for d in range(TENSORS - 1):
        norm = norm + norm_t[d]
    norm_send[1] = norm
    for copy in ring_share(2, 0, norm_send.at[1], norm_y):
        copy.wait_recv()
    norm = norm_send[1] + norm_y[0] + norm_y[1] + norm_y[2]
    norm_send[2] = norm
    for copy in ring_share(3, 1, norm_send.at[2], norm_z):
        copy.wait_recv()
    norm = jnp.sqrt(norm_send[2] + norm_z[0] + norm_z[1] + norm_z[2])
    factor = jnp.minimum(1.0, clip_norm / (norm + 1e-06))[0:1, 0:1]

    bias_one, bias_two = scal[2], scal[3]
    for load in loads[1:]:
        load.wait()
    for copy in chunk_copies:
        copy.wait_recv()
    half = ALL_COLS // 2
    for h in range(2):
        cols = pl.ds(half * h, half)
        summed = jnp.concatenate([decode(chunk_recv[4 * h + j], 16 * SUM_MAX) for j in range(4)], axis=1)
        new, one, two = adam(pm[:, cols], p1[:, cols], p2[:, cols], summed * factor, bias_one, bias_two, weight_decay)
        om[:, cols] = new
        o1[:, cols] = one
        o2[:, cols] = two
        smooth = decay_rate * pa[:, cols] + (1.0 - decay_rate) * new
        for j in range(4):
            wchunk_send[4 * h + j] = new[:, COLS * j : COLS * (j + 1)].astype(jnp.bfloat16)
            achunk_send[4 * h + j] = encode(smooth[:, COLS * j : COLS * (j + 1)], AVERAGE_MAX)
    wchunk_recv[t] = wchunk_send[t]
    achunk_recv[t] = achunk_send[t]
    wchunk_copies = exchange(2, wchunk_send, wchunk_recv)
    achunk_copies = exchange(3, achunk_send, achunk_recv)
    stores = []
    for i, (src, dst) in enumerate(((om, master_out), (o1, one_out), (o2, two_out))):
        store = pltpu.make_async_copy(src, dst, store_sem.at[i])
        store.start()
        stores.append(store)

    new, one, two = adam(
        small_all[1:2], small_all[2:3], small_all[3:4], small_sum * factor, bias_one, bias_two, 0.0
    )
    smooth = decay_rate * small_all[4:5] + (1.0 - decay_rate) * new
    small_out[0:1] = new
    small_out[1:2] = one
    small_out[2:3] = two
    small_out[3:4] = smooth
    small_out[4:8] = jnp.zeros((4, LANES), jnp.float32)

    for copy in wchunk_copies:
        copy.wait_recv()
    rows = jnp.concatenate([wchunk_recv[j].astype(jnp.float32) for j in range(TENSORS)], axis=0)
    wall[s] = rows.astype(jnp.bfloat16)
    for copy in achunk_copies:
        copy.wait_recv()
    rows = jnp.concatenate([achunk_recv[j].astype(jnp.int32) for j in range(TENSORS)], axis=0)
    aall[s] = rows.astype(jnp.int16)

    arrays = (wall, aall)
    lanes = [(x, q) for x in range(2) for q in range(4)]

    def gather_send(x, q, shard, index, axis, sign):
        first, width = PARTS[q]
        ref = arrays[x].at[shard, :, pl.ds(first, width)]
        send(
            ref,
            ref,
            ag_send_sem.at[x, q, index],
            ag_recv_sem.at[x, q, index],
            ring_device(axis, wrap(pos[axis], sign, RING)),
        )

    def gather_wait(x, q, shard, index):
        first, width = PARTS[q]
        ref = arrays[x].at[shard, :, pl.ds(first, width)]
        pltpu.make_async_remote_copy(
            src_ref=ref,
            dst_ref=ref,
            send_sem=ag_send_sem.at[x, q, index],
            recv_sem=ag_recv_sem.at[x, q, index],
            device_id=ring_device(0, wrap(pos[0], 1, RING)),
            device_id_type=MESH,
        ).wait_recv()

    def outer(x, q, j, shard):
        axis, sign = axes[q][0], signs[q]
        gather_send(x, q, shard, 3 + 3 * j, axis, sign)
        gather_send(x, q, shard, 4 + 3 * j, axis, -sign)

    def source(q, shift, shift_outer):
        axis, other = axes[q]
        return shard_of(axis, wrap(pos[axis], shift_outer, RING), wrap(pos[other], shift, RING))

    def relay(x, q, j, shift):
        axis, sign = axes[q][0], signs[q]
        shard = source(q, shift, -sign)
        gather_wait(x, q, shard, 3 + 3 * j)
        gather_send(x, q, shard, 5 + 3 * j, axis, sign)

    for x, q in lanes:
        other, sign = axes[q][1], signs[q]
        gather_send(x, q, s, 0, other, sign)
        gather_send(x, q, s, 1, other, -sign)
        outer(x, q, 0, s)
    for x, q in lanes:
        other, sign = axes[q][1], signs[q]
        shard = source(q, -sign, 0)
        gather_wait(x, q, shard, 0)
        gather_send(x, q, shard, 2, other, sign)
        outer(x, q, 1, shard)
        relay(x, q, 0, 0)
    for x, q in lanes:
        sign = signs[q]
        shard = source(q, sign, 0)
        gather_wait(x, q, shard, 1)
        outer(x, q, 2, shard)
        relay(x, q, 1, -sign)
    for x, q in lanes:
        sign = signs[q]
        shard = source(q, 2, 0)
        gather_wait(x, q, shard, 2)
        outer(x, q, 3, shard)
        relay(x, q, 2, sign)
    for x, q in lanes:
        relay(x, q, 3, 2)
    for x, q in lanes:
        sign = signs[q]
        for j, shift in enumerate((0, -sign, sign, 2)):
            gather_wait(x, q, source(q, shift, sign), 4 + 3 * j)
            gather_wait(x, q, source(q, shift, 2), 5 + 3 * j)
    for i, (src, dst) in enumerate(((wall, weights_out), (aall, codes_out))):
        store = pltpu.make_async_copy(src, dst, store_sem.at[3 + i])
        store.start()
        stores.append(store)
    for copy in pending:
        copy.wait_send()
    for store in stores:
        store.wait()


def communicate(scal, small_in, grads, master, one, two, average):
    hbm = pl.BlockSpec(memory_space=pl.ANY)
    vmem = pl.BlockSpec(memory_space=pltpu.VMEM)
    f32, bf16, i16 = jnp.float32, jnp.bfloat16, jnp.int16
    rows = jax.ShapeDtypeStruct((MINE, ALL_COLS), f32)
    widths = [w for _, w in PARTS]
    chunk = (TENSORS, MINE, COLS)
    return pl.pallas_call(
        step_kernel,
        out_shape=(
            rows,
            rows,
            rows,
            jax.ShapeDtypeStruct((8, LANES), f32),
            jax.ShapeDtypeStruct((SHARDS, ROWS, COLS), bf16),
            jax.ShapeDtypeStruct((SHARDS, ROWS, COLS), i16),
        ),
        in_specs=[pl.BlockSpec(memory_space=pltpu.SMEM), vmem] + [hbm] * 5,
        out_specs=(hbm, hbm, hbm, vmem, hbm, hbm),
        scratch_shapes=[
            pltpu.VMEM((2, SHARDS, ROWS, COLS), bf16),
            *[pltpu.VMEM((MINE, ALL_COLS), f32)] * 7,
            [pltpu.VMEM((3, RING, ROWS, w), i16) for w in widths],
            [pltpu.VMEM((3, RING, ROWS, w), i16) for w in widths],
            [pltpu.VMEM((2, ROWS, w), f32) for w in widths],
            [pltpu.VMEM((3, ROWS, w), i16) for w in widths],
            [pltpu.VMEM((3, ROWS, w), i16) for w in widths],
            pltpu.VMEM((ROWS, COLS), f32),
            pltpu.VMEM(chunk, i16),
            pltpu.VMEM(chunk, i16),
            pltpu.VMEM(chunk, bf16),
            pltpu.VMEM(chunk, bf16),
            pltpu.VMEM(chunk, i16),
            pltpu.VMEM(chunk, i16),
            pltpu.VMEM((3, 8, 128), f32),
            pltpu.VMEM((TENSORS - 1, 8, 128), f32),
            pltpu.VMEM((RING - 1, 8, 128), f32),
            pltpu.VMEM((RING - 1, 8, 128), f32),
            pltpu.VMEM((8, LANES), f32),
            pltpu.VMEM((RING - 1, 8, LANES), f32),
            pltpu.VMEM((RING - 1, 8, LANES), f32),
            pltpu.VMEM((SHARDS, ROWS, COLS), bf16),
            pltpu.VMEM((SHARDS, ROWS, COLS), i16),
            pltpu.SemaphoreType.DMA((5,)),
            pltpu.SemaphoreType.DMA((5,)),
            pltpu.SemaphoreType.DMA((4, 9)),
            pltpu.SemaphoreType.DMA((4, 9)),
            pltpu.SemaphoreType.DMA((4, TENSORS)),
            pltpu.SemaphoreType.DMA((4, TENSORS)),
            pltpu.SemaphoreType.DMA((4, RING - 1)),
            pltpu.SemaphoreType.DMA((4, RING - 1)),
            pltpu.SemaphoreType.DMA((2, 4, 15)),
            pltpu.SemaphoreType.DMA((2, 4, 15)),
        ],
        compiler_params=pltpu.CompilerParams(
            collective_id=0, has_side_effects=True, vmem_limit_bytes=60 * 1024 * 1024
        ),
        name="step",
    )(scal, small_in, grads, master, one, two, average)


def finish_kernel(weights, codes, master, one, two, weights_out, average_out, master_out, one_out, two_out):
    weights_out[...] = weights[...]
    average_out[...] = decode(codes[...], AVERAGE_MAX)

    @pl.when(pl.program_id(0) == 0)
    def _():
        master_out[...] = master[...]
        one_out[...] = one[...]
        two_out[...] = two[...]


def finish(weights, codes, master, one, two):
    block = pl.BlockSpec((2, ROWS, COLS), lambda i: (i, 0, 0))
    whole = pl.BlockSpec((MINE, ALL_COLS), lambda i: (0, 0))
    rows = jax.ShapeDtypeStruct((MINE, ALL_COLS), jnp.float32)
    return pl.pallas_call(
        finish_kernel,
        grid=(SHARDS // 2,),
        in_specs=[block, block, whole, whole, whole],
        out_specs=[block, block, whole, whole, whole],
        out_shape=(
            jax.ShapeDtypeStruct((SHARDS, ROWS, COLS), jnp.bfloat16),
            jax.ShapeDtypeStruct((SHARDS, ROWS, COLS), jnp.float32),
            rows,
            rows,
            rows,
        ),
        name="finish",
    )(weights, codes, master, one, two)


def shards(
    grads,
    small_grads,
    counts,
    step,
    master,
    moment_one,
    moment_two,
    average,
    small_master,
    small_one,
    small_two,
    small_average,
):
    s = lax.axis_index("shard")
    valid = (jnp.arange(2, dtype=jnp.int32) < counts[0]).astype(jnp.float32)
    time = step[0].astype(jnp.float32)
    bias_one = 1.0 - jnp.power(jnp.float32(beta_one), time)
    bias_two = 1.0 - jnp.power(jnp.float32(beta_two), time)
    scal = jnp.stack([valid[0], valid[1], bias_one, bias_two])
    small_term = valid[0] * small_grads[0].astype(jnp.float32) + valid[1] * small_grads[1].astype(jnp.float32)
    state = jnp.concatenate([small_master, small_one, small_two, small_average], axis=0)
    small_in = jnp.zeros((8, LANES), jnp.float32)
    small_in = lax.dynamic_update_slice(small_in, small_term[None], (0, 0))
    small_in = lax.dynamic_update_slice(small_in, state, (1, SEG * s))
    new_master, new_one, new_two, small_new, weights, codes = communicate(
        scal, small_in, grads.reshape(2, SHARDS, ROWS, COLS), master, moment_one, moment_two, average
    )
    weights, averages, new_master, new_one, new_two = finish(weights, codes, new_master, new_one, new_two)
    mine = lax.dynamic_slice(small_new, (0, SEG * s), (3, SEG))
    return (
        new_master,
        new_one,
        new_two,
        mine[0:1],
        mine[1:2],
        mine[2:3],
        weights.reshape(SHARDS * ROWS, COLS),
        small_new[0, :SMALL].astype(jnp.bfloat16),
        averages.reshape(SHARDS * ROWS, COLS),
        small_new[3, :SMALL],
    )


def solution(mesh):
    placed = (
        P("shard", None, "tensor"),
        P("shard", "tensor"),
        P("shard"),
        P(),
        P(("shard", "tensor"), None),
        P(("shard", "tensor"), None),
        P(("shard", "tensor"), None),
        P(("shard", "tensor"), None),
        P("tensor", "shard"),
        P("tensor", "shard"),
        P("tensor", "shard"),
        P("tensor", "shard"),
    )
    return jax.shard_map(
        shards,
        mesh=mesh,
        in_specs=placed,
        out_specs=(
            P(("shard", "tensor"), None),
            P(("shard", "tensor"), None),
            P(("shard", "tensor"), None),
            P("tensor", "shard"),
            P("tensor", "shard"),
            P("tensor", "shard"),
            P(None, "tensor"),
            P("tensor"),
            P(None, "tensor"),
            P("tensor"),
        ),
        check_vma=False,
    )
```

```python
import jax
import jax.numpy as jnp
import numpy as np
from jax import lax
from jax.experimental import pallas as pl
from jax.experimental.pallas import tpu as pltpu
from jax.sharding import PartitionSpec as P

learn_rate = 0.002
beta_one = 0.9
beta_two = 0.999
adam_eps = 1e-08
weight_decay = 0.1
clip_norm = 1.0
decay_rate = 0.99

MESH = pl.DeviceIdType.MESH
RING = 4
SHARDS = RING * RING
TENSORS = 8
ROWS = 56
MINE = 7
COLS = 2080
ALL_COLS = COLS * TENSORS
SMALL = 368
SEG = 23
LANES = 384
PARTS = ((0, 512), (512, 512), (1024, 512), (1536, 544))
TOP = 32700.0
SUM_MAX = 2.0
AVERAGE_MAX = 0.03


def encode(x, most):
    scaled = jnp.abs(x) * (TOP**4 / most) + 1e-20
    root = (lax.rsqrt(lax.rsqrt(scaled)) + 0.5).astype(jnp.int32)
    return jnp.where(x < 0.0, -root, root).astype(jnp.int16)


def decode(code, most):
    root = code.astype(jnp.int32).astype(jnp.float32)
    return (root * root) * (root * jnp.abs(root)) * (most / TOP**4)


def adam(param, first, second, gradient, bias_one, bias_two, decay):
    first_new = beta_one * first + (1.0 - beta_one) * gradient
    second_new = beta_two * second + (1.0 - beta_two) * gradient * gradient
    ratio = first_new / bias_one / (jnp.sqrt(second_new / bias_two) + adam_eps)
    return param - learn_rate * (ratio + decay * param), first_new, second_new


def bias(time, beta):
    total = jnp.float32(0.0)
    for bit in range(10):
        term = ((time >> bit) & 1).astype(jnp.float32) * (1.0 - float(np.float32(beta)) ** (1 << bit))
        total = total + term - total * term
    return total


def place(s, shape, along):
    own = lax.broadcasted_iota(jnp.int32, shape, along)
    every = lax.broadcasted_iota(jnp.int32, shape, 1 - along)
    return jnp.where(jnp.logical_and(every == own + SEG * s, own < SEG), 1.0, 0.0)


def exact_dot(a, b):
    return jnp.dot(a, b, precision=lax.Precision.HIGHEST, preferred_element_type=jnp.float32)


def wrap(position, shift, size):
    return lax.rem(position + (shift + size), size)


def step_kernel(
    counts,
    step,
    small_grads,
    small_master,
    small_one,
    small_two,
    small_average,
    grads_hbm,
    master_hbm,
    one_hbm,
    two_hbm,
    average_hbm,
    om,
    o1,
    o2,
    small_out,
    mine_out,
    wall,
    aall,
    gv,
    loc,
    pm,
    p1,
    p2,
    pa,
    big_send,
    big_recv,
    kept,
    mid_send,
    mid_recv,
    total,
    chunk_send,
    chunk_recv,
    wchunk_send,
    wchunk_recv,
    achunk_send,
    achunk_recv,
    norm_send,
    norm_t,
    norm_y,
    norm_z,
    small_state,
    small_in,
    small_send,
    small_y,
    small_z,
    load_sem,
    rs_send_sem,
    rs_recv_sem,
    t_send_sem,
    t_recv_sem,
    r_send_sem,
    r_recv_sem,
    ag_send_sem,
    ag_recv_sem,
):
    s = lax.axis_index("shard")
    t = lax.axis_index("tensor")
    pos = (lax.div(s, RING), lax.rem(s, RING))
    core_sign = 1 - 2 * lax.rem(t, 2)

    def ring_device(axis, p):
        return (p * RING + pos[1], t) if axis == 0 else (pos[0] * RING + p, t)

    def shard_of(axis, p, k):
        return p * RING + k if axis == 0 else k * RING + p

    loads = []
    for first, width in PARTS:
        cut = (slice(None), pl.ds(first, width))
        loads.append((grads_hbm.at[cut], gv.at[cut]))
    loads += [(master_hbm, pm), (one_hbm, p1), (two_hbm, p2), (average_hbm, pa)]
    loads = [pltpu.make_async_copy(src, dst, load_sem.at[i]) for i, (src, dst) in enumerate(loads)]
    for load in loads:
        load.start()

    valid_one = jnp.minimum(jnp.maximum(counts[0], 0), 1).astype(jnp.float32)
    valid_two = jnp.minimum(jnp.maximum(counts[0] - 1, 0), 1).astype(jnp.float32)
    small_state[...] = jnp.zeros((8, 128), jnp.float32)
    for i, ref in enumerate((small_master, small_one, small_two, small_average)):
        small_state[pl.ds(i + 1, 1), pl.ds(0, SEG)] = ref[...]
    small_in[...] = exact_dot(small_state[...], place(s, (128, LANES), 0))
    micro = small_grads[...].astype(jnp.float32)
    small_in[0:1, pl.ds(0, SMALL)] = valid_one * micro[0:1] + valid_two * micro[1:2]

    barrier = pltpu.get_barrier_semaphore()
    for axis in range(2):
        for d in range(1, RING):
            pl.semaphore_signal(
                barrier, inc=1, device_id=ring_device(axis, wrap(pos[axis], d, RING)), device_id_type=MESH
            )
    for d in range(1, TENSORS):
        pl.semaphore_signal(barrier, inc=1, device_id=(s, wrap(t, d, TENSORS)), device_id_type=MESH)
    pl.semaphore_wait(barrier, 2 * (RING - 1) + TENSORS - 1)

    pending = []

    def send(src, dst, send_sem, recv_sem, device):
        copy = pltpu.make_async_remote_copy(
            src_ref=src, dst_ref=dst, send_sem=send_sem, recv_sem=recv_sem, device_id=device, device_id_type=MESH
        )
        copy.start()
        pending.append(copy)
        return copy

    def ring_share(kind, axis, src, dst):
        return [
            send(
                src,
                dst.at[d - 1],
                r_send_sem.at[kind, d - 1],
                r_recv_sem.at[kind, d - 1],
                ring_device(axis, wrap(pos[axis], d, RING)),
            )
            for d in range(1, RING)
        ]

    small_copies = ring_share(0, 0, small_in, small_y)

    def turn(q, tile):
        first, width = PARTS[q]
        cut = pl.ds(pl.multiple_of(tile * 128, 128), 128)
        a = gv[0, pl.ds(first, width), cut].astype(jnp.float32)
        b = gv[1, pl.ds(first, width), cut].astype(jnp.float32)
        loc[q][cut, :] = (valid_one * a + valid_two * b).T

    def local(shard, q):
        return loc[q][pl.ds(pl.multiple_of(shard * ROWS, 8), ROWS), :]

    axes = ((0, 1), (0, 1), (1, 0), (1, 0))
    signs = (core_sign, -core_sign, core_sign, -core_sign)
    order = [[wrap(pos[axes[q][1]], k, RING) for k in (2, signs[q], -signs[q], 0)] for q in range(4)]
    early = [[None] * 2 for _ in range(4)]
    far = lax.min(lax.div(7 * wrap(pos[0], 2, RING), 4), 4)
    for slot in range(2):
        for q in range(4):
            axis, sign = axes[q][0], signs[q]
            p = pos[axis]
            dest = wrap(p, 2, RING) if slot == 0 else wrap(p, sign, RING)
            if slot == 0:
                loads[q].wait()
            some = (0, 7) if axis == 1 else (0, 3) if slot == 0 else (3, 7)

            def tile(j, carry, q=q, axis=axis):
                turn(q, wrap(far, j, 7) if axis == 0 else j)
                return carry

            if slot == 0 or axis == 0:
                lax.fori_loop(*some, tile, 0)

            def fill(k, carry, q=q, axis=axis, dest=dest, slot=slot):
                big_send[q][slot, k] = encode(local(shard_of(axis, dest, k), q), SUM_MAX)
                return carry

            lax.fori_loop(0, RING, fill, 0)
            to = wrap(p, -sign, RING) if slot == 0 else dest
            early[q][slot] = send(
                big_send[q].at[slot],
                big_recv[q].at[slot],
                rs_send_sem.at[q, slot],
                rs_recv_sem.at[q, slot],
                ring_device(axis, to),
            )
    relayed = [[None] * RING for _ in range(4)]
    for q in range(4):
        early[q][0].wait_recv()
    for i in range(RING):
        for q in range(4):
            axis, sign = axes[q][0], signs[q]
            dest = wrap(pos[axis], -sign, RING)
            k = order[q][i]
            came = decode(big_recv[q][0, k], SUM_MAX)
            big_send[q][2, k] = encode(local(shard_of(axis, dest, k), q) + came, 2 * SUM_MAX)
            relayed[q][i] = send(
                big_send[q].at[2, k],
                big_recv[q].at[2, k],
                rs_send_sem.at[q, 2 + i],
                rs_recv_sem.at[q, 2 + i],
                ring_device(axis, dest),
            )
    for copy in small_copies:
        copy.wait_recv()
    small_send[...] = small_in[...] + small_y[0] + small_y[1] + small_y[2]
    small_copies = ring_share(1, 1, small_send, small_z)
    for q in range(4):
        early[q][1].wait_recv()

    later = [[None] * 3 for _ in range(4)]
    for i in range(RING):
        for q in range(4):
            (axis, other), sign = axes[q], signs[q]
            k = order[q][i]
            relayed[q][i].wait_recv()
            piece = (
                local(shard_of(axis, pos[axis], k), q)
                + decode(big_recv[q][1, k], SUM_MAX)
                + decode(big_recv[q][2, k], 2 * SUM_MAX)
            )
            if i >= 2:
                kept[q][i - 2] = piece
                continue
            mid_send[q][i] = encode(piece, 4 * SUM_MAX)
            to = wrap(pos[other], -sign if i == 0 else sign, RING)
            later[q][i] = send(
                mid_send[q].at[i],
                mid_recv[q].at[i],
                rs_send_sem.at[q, 6 + i],
                rs_recv_sem.at[q, 6 + i],
                ring_device(other, to),
            )
    for q in range(4):
        other, sign = axes[q][1], signs[q]
        later[q][0].wait_recv()
        mid_send[q][2] = encode(kept[q][0] + decode(mid_recv[q][0], 4 * SUM_MAX), 8 * SUM_MAX)
        later[q][2] = send(
            mid_send[q].at[2],
            mid_recv[q].at[2],
            rs_send_sem.at[q, 8],
            rs_recv_sem.at[q, 8],
            ring_device(other, wrap(pos[other], -sign, RING)),
        )
    for copy in small_copies:
        copy.wait_recv()
    small_all = small_send[...] + small_z[0] + small_z[1] + small_z[2]
    small_sum = small_all[0:1]
    squares = jnp.sum(small_sum * small_sum) * (1.0 / SHARDS)
    for q in range(4):
        first, width = PARTS[q]
        later[q][1].wait_recv()
        later[q][2].wait_recv()
        piece = kept[q][1] + decode(mid_recv[q][1], 4 * SUM_MAX) + decode(mid_recv[q][2], 8 * SUM_MAX)
        total[:, pl.ds(first, width)] = piece
        squares = squares + jnp.sum(piece * piece)

    norm_send[0] = jnp.full((8, 128), squares, jnp.float32)
    norm_copies = []
    for d in range(1, TENSORS):
        norm_copies.append(
            send(
                norm_send.at[0],
                norm_t.at[d - 1],
                t_send_sem.at[0, d],
                t_recv_sem.at[0, d],
                (s, wrap(t, d, TENSORS)),
            )
        )
    for j in range(TENSORS):
        chunk_send[j] = encode(total[pl.ds(MINE * j, MINE), :], 16 * SUM_MAX)
    chunk_recv[t] = chunk_send[t]

    def exchange(kind, src, dst):
        copies = []
        for d in range(1, TENSORS):
            to = wrap(t, d, TENSORS)
            copies.append(
                send(src.at[to], dst.at[t], t_send_sem.at[kind, d], t_recv_sem.at[kind, d], (s, to))
            )
        return copies

    chunk_copies = exchange(1, chunk_send, chunk_recv)
    for copy in norm_copies:
        copy.wait_recv()
    norm = norm_send[0]
    for d in range(TENSORS - 1):
        norm = norm + norm_t[d]
    norm_send[1] = norm
    for copy in ring_share(2, 0, norm_send.at[1], norm_y):
        copy.wait_recv()
    norm = norm_send[1] + norm_y[0] + norm_y[1] + norm_y[2]
    norm_send[2] = norm
    for copy in ring_share(3, 1, norm_send.at[2], norm_z):
        copy.wait_recv()
    norm = jnp.sqrt(norm_send[2] + norm_z[0] + norm_z[1] + norm_z[2])
    factor = jnp.minimum(1.0, clip_norm / (norm + 1e-06))[0:1, 0:1]

    bias_one, bias_two = bias(step[0], beta_one), bias(step[0], beta_two)
    for load in loads[4:]:
        load.wait()
    for copy in chunk_copies:
        copy.wait_recv()
    half = ALL_COLS // 2
    for h in range(2):
        cols = pl.ds(half * h, half)
        summed = jnp.concatenate([decode(chunk_recv[4 * h + j], 16 * SUM_MAX) for j in range(4)], axis=1)
        new, one, two = adam(pm[:, cols], p1[:, cols], p2[:, cols], summed * factor, bias_one, bias_two, weight_decay)
        om[:, cols] = new
        o1[:, cols] = one
        o2[:, cols] = two
        smooth = decay_rate * pa[:, cols] + (1.0 - decay_rate) * new
        for j in range(4):
            wchunk_send[4 * h + j] = new[:, COLS * j : COLS * (j + 1)].astype(jnp.bfloat16)
            achunk_send[4 * h + j] = encode(smooth[:, COLS * j : COLS * (j + 1)], AVERAGE_MAX)
    wchunk_recv[t] = wchunk_send[t]
    achunk_recv[t] = achunk_send[t]
    wchunk_copies = exchange(2, wchunk_send, wchunk_recv)
    achunk_copies = exchange(3, achunk_send, achunk_recv)

    new, one, two = adam(
        small_all[1:2], small_all[2:3], small_all[3:4], small_sum * factor, bias_one, bias_two, 0.0
    )
    smooth = decay_rate * small_all[4:5] + (1.0 - decay_rate) * new
    small_out[0:1] = new
    small_out[1:2] = one
    small_out[2:3] = two
    small_out[3:4] = smooth
    small_out[4:8] = jnp.zeros((4, LANES), jnp.float32)
    mine_out[...] = exact_dot(small_out[...], place(s, (LANES, 128), 1))

    for copy in wchunk_copies:
        copy.wait_recv()
    rows = jnp.concatenate([wchunk_recv[j].astype(jnp.float32) for j in range(TENSORS)], axis=0)
    wall[s] = rows.astype(jnp.bfloat16)
    for copy in achunk_copies:
        copy.wait_recv()
    rows = jnp.concatenate([achunk_recv[j].astype(jnp.int32) for j in range(TENSORS)], axis=0)
    aall[s] = rows.astype(jnp.int16)

    arrays = (wall, aall)
    lanes = [(x, q) for x in range(2) for q in range(4)]

    def gather_send(x, q, shard, index, axis, sign):
        first, width = PARTS[q]
        ref = arrays[x].at[shard, :, pl.ds(first, width)]
        send(
            ref,
            ref,
            ag_send_sem.at[x, q, index],
            ag_recv_sem.at[x, q, index],
            ring_device(axis, wrap(pos[axis], sign, RING)),
        )

    def gather_wait(x, q, shard, index):
        first, width = PARTS[q]
        ref = arrays[x].at[shard, :, pl.ds(first, width)]
        pltpu.make_async_remote_copy(
            src_ref=ref,
            dst_ref=ref,
            send_sem=ag_send_sem.at[x, q, index],
            recv_sem=ag_recv_sem.at[x, q, index],
            device_id=ring_device(0, wrap(pos[0], 1, RING)),
            device_id_type=MESH,
        ).wait_recv()

    def outer(x, q, j, shard):
        axis, sign = axes[q][0], signs[q]
        gather_send(x, q, shard, 3 + 3 * j, axis, sign)
        gather_send(x, q, shard, 4 + 3 * j, axis, -sign)

    def source(q, shift, shift_outer):
        axis, other = axes[q]
        return shard_of(axis, wrap(pos[axis], shift_outer, RING), wrap(pos[other], shift, RING))

    def relay(x, q, j, shift):
        axis, sign = axes[q][0], signs[q]
        shard = source(q, shift, -sign)
        gather_wait(x, q, shard, 3 + 3 * j)
        gather_send(x, q, shard, 5 + 3 * j, axis, sign)

    for x, q in lanes:
        other, sign = axes[q][1], signs[q]
        gather_send(x, q, s, 0, other, sign)
        gather_send(x, q, s, 1, other, -sign)
        outer(x, q, 0, s)
    for x, q in lanes:
        other, sign = axes[q][1], signs[q]
        shard = source(q, -sign, 0)
        gather_wait(x, q, shard, 0)
        gather_send(x, q, shard, 2, other, sign)
        outer(x, q, 1, shard)
        relay(x, q, 0, 0)
    for x, q in lanes:
        sign = signs[q]
        shard = source(q, sign, 0)
        gather_wait(x, q, shard, 1)
        outer(x, q, 2, shard)
        relay(x, q, 1, -sign)
    for x, q in lanes:
        sign = signs[q]
        shard = source(q, 2, 0)
        gather_wait(x, q, shard, 2)
        outer(x, q, 3, shard)
        relay(x, q, 2, sign)
    for x, q in lanes:
        relay(x, q, 3, 2)
    for x, q in lanes:
        sign = signs[q]
        for j, shift in enumerate((0, -sign, sign, 2)):
            gather_wait(x, q, source(q, shift, sign), 4 + 3 * j)
            gather_wait(x, q, source(q, shift, 2), 5 + 3 * j)
    for copy in pending:
        copy.wait_send()


def communicate(*args):
    hbm = pl.BlockSpec(memory_space=pl.ANY)
    vmem = pl.BlockSpec(memory_space=pltpu.VMEM)
    smem = pl.BlockSpec(memory_space=pltpu.SMEM)
    f32, bf16, i16 = jnp.float32, jnp.bfloat16, jnp.int16
    widths = [w for _, w in PARTS]
    chunk = (TENSORS, MINE, COLS)
    return pl.pallas_call(
        step_kernel,
        out_shape=(
            *[pltpu.VMEM((MINE, ALL_COLS), f32)] * 3,
            pltpu.VMEM((8, LANES), f32),
            pltpu.VMEM((8, 128), f32),
            pltpu.VMEM((SHARDS, ROWS, COLS), bf16),
            pltpu.VMEM((SHARDS, ROWS, COLS), i16),
        ),
        in_specs=[smem] * 2 + [vmem] * 5 + [hbm] * 5,
        out_specs=(vmem,) * 7,
        scratch_shapes=[
            pltpu.VMEM((2, COLS, SHARDS * ROWS), bf16),
            [pltpu.VMEM((SHARDS * ROWS, w), f32) for w in widths],
            *[pltpu.VMEM((MINE, ALL_COLS), f32)] * 4,
            [pltpu.VMEM((3, RING, ROWS, w), i16) for w in widths],
            [pltpu.VMEM((3, RING, ROWS, w), i16) for w in widths],
            [pltpu.VMEM((2, ROWS, w), f32) for w in widths],
            [pltpu.VMEM((3, ROWS, w), i16) for w in widths],
            [pltpu.VMEM((3, ROWS, w), i16) for w in widths],
            pltpu.VMEM((ROWS, COLS), f32),
            pltpu.VMEM(chunk, i16),
            pltpu.VMEM(chunk, i16),
            pltpu.VMEM(chunk, bf16),
            pltpu.VMEM(chunk, bf16),
            pltpu.VMEM(chunk, i16),
            pltpu.VMEM(chunk, i16),
            pltpu.VMEM((3, 8, 128), f32),
            pltpu.VMEM((TENSORS - 1, 8, 128), f32),
            pltpu.VMEM((RING - 1, 8, 128), f32),
            pltpu.VMEM((RING - 1, 8, 128), f32),
            pltpu.VMEM((8, 128), f32),
            pltpu.VMEM((8, LANES), f32),
            pltpu.VMEM((8, LANES), f32),
            pltpu.VMEM((RING - 1, 8, LANES), f32),
            pltpu.VMEM((RING - 1, 8, LANES), f32),
            pltpu.SemaphoreType.DMA((8,)),
            pltpu.SemaphoreType.DMA((4, 9)),
            pltpu.SemaphoreType.DMA((4, 9)),
            pltpu.SemaphoreType.DMA((4, TENSORS)),
            pltpu.SemaphoreType.DMA((4, TENSORS)),
            pltpu.SemaphoreType.DMA((4, RING - 1)),
            pltpu.SemaphoreType.DMA((4, RING - 1)),
            pltpu.SemaphoreType.DMA((2, 4, 15)),
            pltpu.SemaphoreType.DMA((2, 4, 15)),
        ],
        compiler_params=pltpu.CompilerParams(
            collective_id=0, has_side_effects=True, vmem_limit_bytes=48 * 1024 * 1024
        ),
        name="step",
    )(*args)


TURN = 256


def finish_kernel(
    weights,
    codes,
    master,
    one,
    two,
    small,
    mine,
    weights_out,
    average_out,
    master_out,
    one_out,
    two_out,
    small_out,
    small_one_out,
    small_two_out,
    small_weights_out,
    small_average_out,
):
    step = pl.program_id(0)
    last = COLS // TURN

    def turn(width, first):
        cut = (slice(None), slice(None), pl.ds(first, width))
        weights_out[pl.ds(0, width), :] = weights[cut].reshape(SHARDS * ROWS, width).T
        code = codes[cut].astype(jnp.int32).reshape(SHARDS * ROWS, width).T
        average_out[pl.ds(0, width), :] = decode(code, AVERAGE_MAX)

    @pl.when(step < last)
    def _():
        turn(TURN, pl.multiple_of(step * TURN, TURN))

    @pl.when(step == last)
    def _():
        turn(COLS - last * TURN, last * TURN)

    @pl.when(step == 0)
    def _():
        master_out[...] = master[...]
        one_out[...] = one[...]
        two_out[...] = two[...]
        small_out[...] = mine[0:1, 0:SEG]
        small_one_out[...] = mine[1:2, 0:SEG]
        small_two_out[...] = mine[2:3, 0:SEG]
        small_weights_out[...] = small[0:1, 0:SMALL].astype(jnp.bfloat16)
        small_average_out[...] = small[3:4, 0:SMALL]


def finish(weights, codes, master, one, two, small, mine):
    def whole(*shape):
        return pl.BlockSpec(shape, lambda i: (0,) * len(shape))

    vmem = pl.BlockSpec(memory_space=pltpu.VMEM)
    f32, bf16 = jnp.float32, jnp.bfloat16
    rows = jax.ShapeDtypeStruct((MINE, ALL_COLS), f32)
    few = jax.ShapeDtypeStruct((1, SEG), f32)
    turned = pl.BlockSpec((TURN, SHARDS * ROWS), lambda i: (i, 0))
    return pl.pallas_call(
        finish_kernel,
        grid=(pl.cdiv(COLS, TURN),),
        in_specs=[vmem] * 7,
        out_specs=[turned, turned] + [whole(MINE, ALL_COLS)] * 3 + [whole(1, SEG)] * 3 + [whole(1, SMALL)] * 2,
        out_shape=(
            jax.ShapeDtypeStruct((COLS, SHARDS * ROWS), bf16),
            jax.ShapeDtypeStruct((COLS, SHARDS * ROWS), f32),
            rows,
            rows,
            rows,
            few,
            few,
            few,
            jax.ShapeDtypeStruct((1, SMALL), bf16),
            jax.ShapeDtypeStruct((1, SMALL), f32),
        ),
        compiler_params=pltpu.CompilerParams(vmem_limit_bytes=32 * 1024 * 1024),
        name="finish",
    )(weights, codes, master, one, two, small, mine)


def shards(
    grads,
    small_grads,
    counts,
    step,
    master,
    moment_one,
    moment_two,
    average,
    small_master,
    small_one,
    small_two,
    small_average,
):
    new_master, new_one, new_two, small, mine, weights, codes = communicate(
        counts,
        step,
        small_grads,
        small_master,
        small_one,
        small_two,
        small_average,
        grads.transpose(0, 2, 1),
        master,
        moment_one,
        moment_two,
        average,
    )
    (weights, averages, new_master, new_one, new_two, small_new, small_new_one, small_new_two, small_weights, small_averages) = finish(
        weights, codes, new_master, new_one, new_two, small, mine
    )
    return (
        new_master,
        new_one,
        new_two,
        small_new,
        small_new_one,
        small_new_two,
        weights.T,
        small_weights.reshape(SMALL),
        averages.T,
        small_averages.reshape(SMALL),
    )


def solution(mesh):
    placed = (
        P("shard", None, "tensor"),
        P("shard", "tensor"),
        P("shard"),
        P(),
        P(("shard", "tensor"), None),
        P(("shard", "tensor"), None),
        P(("shard", "tensor"), None),
        P(("shard", "tensor"), None),
        P("tensor", "shard"),
        P("tensor", "shard"),
        P("tensor", "shard"),
        P("tensor", "shard"),
    )
    return jax.shard_map(
        shards,
        mesh=mesh,
        in_specs=placed,
        out_specs=(
            P(("shard", "tensor"), None),
            P(("shard", "tensor"), None),
            P(("shard", "tensor"), None),
            P("tensor", "shard"),
            P("tensor", "shard"),
            P("tensor", "shard"),
            P(None, "tensor"),
            P("tensor"),
            P(None, "tensor"),
            P("tensor"),
        ),
        check_vma=False,
    )
```

```python
import jax
import jax.numpy as jnp
import numpy as np
from jax import lax
from jax.experimental import pallas as pl
from jax.experimental.pallas import tpu as pltpu
from jax.sharding import PartitionSpec as P

learn_rate = 0.002
beta_one = 0.9
beta_two = 0.999
adam_eps = 1e-08
weight_decay = 0.1
clip_norm = 1.0
decay_rate = 0.99

MESH = pl.DeviceIdType.MESH
RING = 4
SHARDS = RING * RING
TENSORS = 8
ROWS = 56
MINE = 7
COLS = 2080
ALL_COLS = COLS * TENSORS
SMALL = 368
SEG = 23
LANES = 384
PARTS = ((0, 512), (512, 512), (1024, 512), (1536, 544))
TOP = 32700.0
SUM_MAX = 2.0
AVERAGE_MAX = 0.02
WEIGHT_UNIT = 2.0**-33


def encode(x, most):
    scaled = jnp.abs(x) * (TOP**4 / most) + 1e-20
    root = (lax.rsqrt(lax.rsqrt(scaled)) + 0.5).astype(jnp.int32)
    return jnp.where(x < 0.0, -root, root).astype(jnp.int16)


def decode(code, most):
    root = code.astype(jnp.int32).astype(jnp.float32)
    return (root * root) * (root * jnp.abs(root)) * (most / TOP**4)


def encode_weight(x):
    units = jnp.minimum(jnp.abs(x) * (1.0 / WEIGHT_UNIT), 2147483520.0)
    whole = units.astype(jnp.int32)
    shift = jnp.zeros_like(whole)
    for bits in (16, 8, 4, 2, 1):
        shift = shift + jnp.where((whole >> shift) >= (1 << (bits + 10)), bits, 0)
    kept = whole >> shift
    cut = jnp.logical_or((kept << shift) != whole, whole.astype(jnp.float32) != units)
    code = ((shift << 10) + kept) | jnp.where(cut, 1, 0)
    return jnp.where(x < 0.0, -code, code).astype(jnp.int16)


def decode_weight(code):
    code = code.astype(jnp.int32)
    size = jnp.abs(code)
    shift = jnp.maximum((size >> 10) - 1, 0)
    value = ((size - (shift << 10)) << shift).astype(jnp.float32)
    return jnp.where(code < 0, -WEIGHT_UNIT, WEIGHT_UNIT) * value


def adam(param, first, second, gradient, bias_one, bias_two, decay):
    first_new = beta_one * first + (1.0 - beta_one) * gradient
    second_new = beta_two * second + (1.0 - beta_two) * gradient * gradient
    ratio = first_new / bias_one / (jnp.sqrt(second_new / bias_two) + adam_eps)
    return param - learn_rate * (ratio + decay * param), first_new, second_new


def bias(time, beta):
    total = jnp.float32(0.0)
    for bit in range(10):
        term = ((time >> bit) & 1).astype(jnp.float32) * (1.0 - float(np.float32(beta)) ** (1 << bit))
        total = total + term - total * term
    return total


def place(s, shape, along):
    own = lax.broadcasted_iota(jnp.int32, shape, along)
    every = lax.broadcasted_iota(jnp.int32, shape, 1 - along)
    return jnp.where(jnp.logical_and(every == own + SEG * s, own < SEG), 1.0, 0.0)


def exact_dot(a, b):
    return jnp.dot(a, b, precision=lax.Precision.HIGHEST, preferred_element_type=jnp.float32)


def wrap(position, shift, size):
    return lax.rem(position + (shift + size), size)


def step_kernel(
    counts,
    step,
    small_grads,
    small_master,
    small_one,
    small_two,
    small_average,
    grads_hbm,
    master_hbm,
    one_hbm,
    two_hbm,
    average_hbm,
    om,
    o1,
    o2,
    small_out,
    mine_out,
    wall,
    smooth_out,
    gv,
    loc,
    pm,
    p1,
    p2,
    pa,
    big_send,
    big_recv,
    kept,
    mid_send,
    mid_recv,
    total,
    chunk_send,
    chunk_recv,
    wchunk_send,
    wchunk_recv,
    achunk_send,
    achunk_recv,
    aall,
    norm_send,
    norm_t,
    norm_y,
    norm_z,
    small_state,
    small_in,
    small_send,
    small_y,
    small_z,
    load_sem,
    rs_send_sem,
    rs_recv_sem,
    t_send_sem,
    t_recv_sem,
    r_send_sem,
    r_recv_sem,
    ag_send_sem,
    ag_recv_sem,
):
    s = lax.axis_index("shard")
    t = lax.axis_index("tensor")
    pos = (lax.div(s, RING), lax.rem(s, RING))
    core_sign = 1 - 2 * lax.rem(t, 2)

    def ring_device(axis, p):
        return (p * RING + pos[1], t) if axis == 0 else (pos[0] * RING + p, t)

    def shard_of(axis, p, k):
        return p * RING + k if axis == 0 else k * RING + p

    loads = [(average_hbm, pa)]
    for first, width in PARTS:
        cut = (slice(None), pl.ds(first, width))
        loads.append((grads_hbm.at[cut], gv.at[cut]))
    loads += [(master_hbm, pm), (one_hbm, p1), (two_hbm, p2)]
    loads = [pltpu.make_async_copy(src, dst, load_sem.at[i]) for i, (src, dst) in enumerate(loads)]
    for load in loads:
        load.start()

    valid_one = jnp.minimum(jnp.maximum(counts[0], 0), 1).astype(jnp.float32)
    valid_two = jnp.minimum(jnp.maximum(counts[0] - 1, 0), 1).astype(jnp.float32)
    small_state[...] = jnp.zeros((8, 128), jnp.float32)
    for i, ref in enumerate((small_master, small_one, small_two, small_average)):
        small_state[pl.ds(i + 1, 1), pl.ds(0, SEG)] = ref[...]
    small_in[...] = exact_dot(small_state[...], place(s, (128, LANES), 0))
    micro = small_grads[...].astype(jnp.float32)
    small_in[0:1, pl.ds(0, SMALL)] = valid_one * micro[0:1] + valid_two * micro[1:2]

    barrier = pltpu.get_barrier_semaphore()
    for axis in range(2):
        for d in range(1, RING):
            pl.semaphore_signal(
                barrier, inc=1, device_id=ring_device(axis, wrap(pos[axis], d, RING)), device_id_type=MESH
            )
    for d in range(1, TENSORS):
        pl.semaphore_signal(barrier, inc=1, device_id=(s, wrap(t, d, TENSORS)), device_id_type=MESH)
    pl.semaphore_wait(barrier, 2 * (RING - 1) + TENSORS - 1)

    pending = []

    def send(src, dst, send_sem, recv_sem, device):
        copy = pltpu.make_async_remote_copy(
            src_ref=src, dst_ref=dst, send_sem=send_sem, recv_sem=recv_sem, device_id=device, device_id_type=MESH
        )
        copy.start()
        pending.append(copy)
        return copy

    def ring_share(kind, axis, src, dst):
        return [
            send(
                src,
                dst.at[d - 1],
                r_send_sem.at[kind, d - 1],
                r_recv_sem.at[kind, d - 1],
                ring_device(axis, wrap(pos[axis], d, RING)),
            )
            for d in range(1, RING)
        ]

    def exchange(kind, src, dst):
        copies = []
        for d in range(1, TENSORS):
            to = wrap(t, d, TENSORS)
            copies.append(
                send(src.at[to], dst.at[t], t_send_sem.at[kind, d], t_recv_sem.at[kind, d], (s, to))
            )
        return copies

    loads[0].wait()
    half = ALL_COLS // 2
    for h in range(2):
        codes = pa[:, pl.ds(half * h, half)]
        for j in range(4):
            achunk_send[4 * h + j] = encode(codes[:, COLS * j : COLS * (j + 1)], AVERAGE_MAX)
    achunk_recv[t] = achunk_send[t]
    achunk_copies = exchange(3, achunk_send, achunk_recv)

    small_copies = ring_share(0, 0, small_in, small_y)

    def turn(q, tile):
        first, width = PARTS[q]
        cut = pl.ds(pl.multiple_of(tile * 128, 128), 128)
        a = gv[0, pl.ds(first, width), cut].astype(jnp.float32)
        b = gv[1, pl.ds(first, width), cut].astype(jnp.float32)
        loc[q][cut, :] = (valid_one * a + valid_two * b).T

    def local(shard, q):
        return loc[q][pl.ds(pl.multiple_of(shard * ROWS, 8), ROWS), :]

    axes = ((0, 1), (0, 1), (1, 0), (1, 0))
    signs = (core_sign, -core_sign, core_sign, -core_sign)
    order = [[wrap(pos[axes[q][1]], k, RING) for k in (2, signs[q], -signs[q], 0)] for q in range(4)]
    arrays = (wall, aall)

    def gather_send(x, q, shard, index, axis, sign):
        first, width = PARTS[q]
        ref = arrays[x].at[shard, :, pl.ds(first, width)]
        send(
            ref,
            ref,
            ag_send_sem.at[x, q, index],
            ag_recv_sem.at[x, q, index],
            ring_device(axis, wrap(pos[axis], sign, RING)),
        )

    def gather_wait(x, q, shard, index):
        first, width = PARTS[q]
        ref = arrays[x].at[shard, :, pl.ds(first, width)]
        pltpu.make_async_remote_copy(
            src_ref=ref,
            dst_ref=ref,
            send_sem=ag_send_sem.at[x, q, index],
            recv_sem=ag_recv_sem.at[x, q, index],
            device_id=ring_device(0, wrap(pos[0], 1, RING)),
            device_id_type=MESH,
        ).wait_recv()

    def outer(x, q, j, shard):
        axis, sign = axes[q][0], signs[q]
        gather_send(x, q, shard, 3 + 3 * j, axis, sign)
        gather_send(x, q, shard, 4 + 3 * j, axis, -sign)

    def source(q, shift, shift_outer):
        axis, other = axes[q]
        return shard_of(axis, wrap(pos[axis], shift_outer, RING), wrap(pos[other], shift, RING))

    def relay(x, q, j, shift):
        axis, sign = axes[q][0], signs[q]
        shard = source(q, shift, -sign)
        gather_wait(x, q, shard, 3 + 3 * j)
        gather_send(x, q, shard, 5 + 3 * j, axis, sign)

    def gather_first(x, q):
        other, sign = axes[q][1], signs[q]
        gather_send(x, q, s, 0, other, sign)
        gather_send(x, q, s, 1, other, -sign)
        outer(x, q, 0, s)

    def gather_second(x, q):
        other, sign = axes[q][1], signs[q]
        shard = source(q, -sign, 0)
        gather_wait(x, q, shard, 0)
        gather_send(x, q, shard, 2, other, sign)
        outer(x, q, 1, shard)
        relay(x, q, 0, 0)

    def gather_third(x, q):
        sign = signs[q]
        shard = source(q, sign, 0)
        gather_wait(x, q, shard, 1)
        outer(x, q, 2, shard)
        relay(x, q, 1, -sign)

    def gather_fourth(x, q):
        sign = signs[q]
        shard = source(q, 2, 0)
        gather_wait(x, q, shard, 2)
        outer(x, q, 3, shard)
        relay(x, q, 2, sign)

    def gather_fifth(x, q):
        relay(x, q, 3, 2)

    def gather_end(x, q):
        sign = signs[q]
        for j, shift in enumerate((0, -sign, sign, 2)):
            gather_wait(x, q, source(q, shift, sign), 4 + 3 * j)
            gather_wait(x, q, source(q, shift, 2), 5 + 3 * j)

    def turn_average(q):
        first, width = PARTS[q]
        for c in range(0, width, 128):
            some = min(128, width - c)
            codes = aall[:, :, pl.ds(first + c, some)].astype(jnp.int32).reshape(SHARDS * ROWS, some)
            smooth_out[pl.ds(first + c, some), :] = decay_rate * decode(codes.T, AVERAGE_MAX)

    early = [[None] * 2 for _ in range(4)]
    far = lax.min(lax.div(7 * wrap(pos[0], 2, RING), 4), 4)
    for slot in range(2):
        for q in range(4):
            axis, sign = axes[q][0], signs[q]
            p = pos[axis]
            dest = wrap(p, 2, RING) if slot == 0 else wrap(p, sign, RING)
            if slot == 0:
                loads[q + 1].wait()
            some = (0, 7) if axis == 1 else (0, 3) if slot == 0 else (3, 7)

            def tile(j, carry, q=q, axis=axis):
                turn(q, wrap(far, j, 7) if axis == 0 else j)
                return carry

            if slot == 0 or axis == 0:
                lax.fori_loop(*some, tile, 0)

            def fill(k, carry, q=q, axis=axis, dest=dest, slot=slot):
                big_send[q][slot, k] = encode(local(shard_of(axis, dest, k), q), SUM_MAX)
                return carry

            lax.fori_loop(0, RING, fill, 0)
            to = wrap(p, -sign, RING) if slot == 0 else dest
            early[q][slot] = send(
                big_send[q].at[slot],
                big_recv[q].at[slot],
                rs_send_sem.at[q, slot],
                rs_recv_sem.at[q, slot],
                ring_device(axis, to),
            )
    relayed = [[None] * RING for _ in range(4)]
    for q in range(4):
        early[q][0].wait_recv()
    for i in range(RING):
        for q in range(4):
            axis, sign = axes[q][0], signs[q]
            dest = wrap(pos[axis], -sign, RING)
            k = order[q][i]
            came = decode(big_recv[q][0, k], SUM_MAX)
            big_send[q][2, k] = encode(local(shard_of(axis, dest, k), q) + came, 2 * SUM_MAX)
            relayed[q][i] = send(
                big_send[q].at[2, k],
                big_recv[q].at[2, k],
                rs_send_sem.at[q, 2 + i],
                rs_recv_sem.at[q, 2 + i],
                ring_device(axis, dest),
            )
    for copy in small_copies:
        copy.wait_recv()
    small_send[...] = small_in[...] + small_y[0] + small_y[1] + small_y[2]
    small_copies = ring_share(1, 1, small_send, small_z)
    for q in range(4):
        early[q][1].wait_recv()
    for copy in achunk_copies:
        copy.wait_recv()
    aall[s] = jnp.concatenate([achunk_recv[j].astype(jnp.int32) for j in range(TENSORS)], axis=0).astype(jnp.int16)

    later = [[None] * 3 for _ in range(4)]
    for i in range(RING):
        for q in range(4):
            (axis, other), sign = axes[q], signs[q]
            k = order[q][i]
            relayed[q][i].wait_recv()
            piece = (
                local(shard_of(axis, pos[axis], k), q)
                + decode(big_recv[q][1, k], SUM_MAX)
                + decode(big_recv[q][2, k], 2 * SUM_MAX)
            )
            if i >= 2:
                kept[q][i - 2] = piece
                continue
            mid_send[q][i] = encode(piece, 4 * SUM_MAX)
            to = wrap(pos[other], -sign if i == 0 else sign, RING)
            later[q][i] = send(
                mid_send[q].at[i],
                mid_recv[q].at[i],
                rs_send_sem.at[q, 6 + i],
                rs_recv_sem.at[q, 6 + i],
                ring_device(other, to),
            )
    for q in range(4):
        other, sign = axes[q][1], signs[q]
        later[q][0].wait_recv()
        mid_send[q][2] = encode(kept[q][0] + decode(mid_recv[q][0], 4 * SUM_MAX), 8 * SUM_MAX)
        later[q][2] = send(
            mid_send[q].at[2],
            mid_recv[q].at[2],
            rs_send_sem.at[q, 8],
            rs_recv_sem.at[q, 8],
            ring_device(other, wrap(pos[other], -sign, RING)),
        )
    for q in range(4):
        gather_first(1, q)
    for copy in small_copies:
        copy.wait_recv()
    small_all = small_send[...] + small_z[0] + small_z[1] + small_z[2]
    small_sum = small_all[0:1]
    squares = jnp.sum(small_sum * small_sum) * (1.0 / SHARDS)
    for q in range(4):
        first, width = PARTS[q]
        later[q][1].wait_recv()
        later[q][2].wait_recv()
        piece = kept[q][1] + decode(mid_recv[q][1], 4 * SUM_MAX) + decode(mid_recv[q][2], 8 * SUM_MAX)
        total[:, pl.ds(first, width)] = piece
        squares = squares + jnp.sum(piece * piece)

    norm_send[0] = jnp.full((8, 128), squares, jnp.float32)
    norm_copies = []
    for d in range(1, TENSORS):
        norm_copies.append(
            send(
                norm_send.at[0],
                norm_t.at[d - 1],
                t_send_sem.at[0, d],
                t_recv_sem.at[0, d],
                (s, wrap(t, d, TENSORS)),
            )
        )
    for j in range(TENSORS):
        chunk_send[j] = encode(total[pl.ds(MINE * j, MINE), :], 16 * SUM_MAX)
    chunk_recv[t] = chunk_send[t]

    chunk_copies = exchange(1, chunk_send, chunk_recv)
    for copy in norm_copies:
        copy.wait_recv()
    norm = norm_send[0]
    for d in range(TENSORS - 1):
        norm = norm + norm_t[d]
    norm_send[1] = norm
    for copy in ring_share(2, 0, norm_send.at[1], norm_y):
        copy.wait_recv()
    norm = norm_send[1] + norm_y[0] + norm_y[1] + norm_y[2]
    norm_send[2] = norm
    norm_copies = ring_share(3, 1, norm_send.at[2], norm_z)
    for q in range(4):
        gather_second(1, q)
    for copy in norm_copies:
        copy.wait_recv()
    norm = jnp.sqrt(norm_send[2] + norm_z[0] + norm_z[1] + norm_z[2])
    factor = jnp.minimum(1.0, clip_norm / (norm + 1e-06))[0:1, 0:1]

    bias_one, bias_two = bias(step[0], beta_one), bias(step[0], beta_two)
    for load in loads[5:]:
        load.wait()
    for copy in chunk_copies:
        copy.wait_recv()
    for h in range(2):
        cols = pl.ds(half * h, half)
        summed = jnp.concatenate([decode(chunk_recv[4 * h + j], 16 * SUM_MAX) for j in range(4)], axis=1)
        new, one, two = adam(pm[:, cols], p1[:, cols], p2[:, cols], summed * factor, bias_one, bias_two, weight_decay)
        om[:, cols] = new
        o1[:, cols] = one
        o2[:, cols] = two
        for j in range(4):
            wchunk_send[4 * h + j] = encode_weight(new[:, COLS * j : COLS * (j + 1)])
    wchunk_recv[t] = wchunk_send[t]
    wchunk_copies = exchange(2, wchunk_send, wchunk_recv)
    for q in range(4):
        gather_third(1, q)

    new, one, two = adam(
        small_all[1:2], small_all[2:3], small_all[3:4], small_sum * factor, bias_one, bias_two, 0.0
    )
    smooth = decay_rate * small_all[4:5] + (1.0 - decay_rate) * new
    small_out[0:1] = new
    small_out[1:2] = one
    small_out[2:3] = two
    small_out[3:4] = smooth
    small_out[4:8] = jnp.zeros((4, LANES), jnp.float32)
    mine_out[...] = exact_dot(small_out[...], place(s, (LANES, 128), 1))

    for q in range(4):
        gather_fourth(1, q)
    for copy in wchunk_copies:
        copy.wait_recv()
    wall[s] = jnp.concatenate([wchunk_recv[j].astype(jnp.int32) for j in range(TENSORS)], axis=0).astype(jnp.int16)
    for q in range(4):
        gather_first(0, q)
    for q in range(4):
        gather_fifth(1, q)
    for q in range(4):
        gather_second(0, q)
    for q in range(4):
        gather_end(1, q)
    turn_average(0)
    for q in range(4):
        gather_third(0, q)
    turn_average(1)
    for q in range(4):
        gather_fourth(0, q)
    turn_average(2)
    for q in range(4):
        gather_fifth(0, q)
    turn_average(3)
    for q in range(4):
        gather_end(0, q)
    for copy in pending:
        copy.wait_send()


def communicate(*args):
    hbm = pl.BlockSpec(memory_space=pl.ANY)
    vmem = pl.BlockSpec(memory_space=pltpu.VMEM)
    smem = pl.BlockSpec(memory_space=pltpu.SMEM)
    f32, bf16, i16 = jnp.float32, jnp.bfloat16, jnp.int16
    widths = [w for _, w in PARTS]
    chunk = (TENSORS, MINE, COLS)
    return pl.pallas_call(
        step_kernel,
        out_shape=(
            *[pltpu.VMEM((MINE, ALL_COLS), f32)] * 3,
            pltpu.VMEM((8, LANES), f32),
            pltpu.VMEM((8, 128), f32),
            pltpu.VMEM((SHARDS, ROWS, COLS), i16),
            pltpu.VMEM((COLS, SHARDS * ROWS), f32),
        ),
        in_specs=[smem] * 2 + [vmem] * 5 + [hbm] * 5,
        out_specs=(vmem,) * 7,
        scratch_shapes=[
            pltpu.VMEM((2, COLS, SHARDS * ROWS), bf16),
            [pltpu.VMEM((SHARDS * ROWS, w), f32) for w in widths],
            *[pltpu.VMEM((MINE, ALL_COLS), f32)] * 4,
            [pltpu.VMEM((3, RING, ROWS, w), i16) for w in widths],
            [pltpu.VMEM((3, RING, ROWS, w), i16) for w in widths],
            [pltpu.VMEM((2, ROWS, w), f32) for w in widths],
            [pltpu.VMEM((3, ROWS, w), i16) for w in widths],
            [pltpu.VMEM((3, ROWS, w), i16) for w in widths],
            pltpu.VMEM((ROWS, COLS), f32),
            pltpu.VMEM(chunk, i16),
            pltpu.VMEM(chunk, i16),
            pltpu.VMEM(chunk, i16),
            pltpu.VMEM(chunk, i16),
            pltpu.VMEM(chunk, i16),
            pltpu.VMEM(chunk, i16),
            pltpu.VMEM((SHARDS, ROWS, COLS), i16),
            pltpu.VMEM((3, 8, 128), f32),
            pltpu.VMEM((TENSORS - 1, 8, 128), f32),
            pltpu.VMEM((RING - 1, 8, 128), f32),
            pltpu.VMEM((RING - 1, 8, 128), f32),
            pltpu.VMEM((8, 128), f32),
            pltpu.VMEM((8, LANES), f32),
            pltpu.VMEM((8, LANES), f32),
            pltpu.VMEM((RING - 1, 8, LANES), f32),
            pltpu.VMEM((RING - 1, 8, LANES), f32),
            pltpu.SemaphoreType.DMA((8,)),
            pltpu.SemaphoreType.DMA((4, 9)),
            pltpu.SemaphoreType.DMA((4, 9)),
            pltpu.SemaphoreType.DMA((4, TENSORS)),
            pltpu.SemaphoreType.DMA((4, TENSORS)),
            pltpu.SemaphoreType.DMA((4, RING - 1)),
            pltpu.SemaphoreType.DMA((4, RING - 1)),
            pltpu.SemaphoreType.DMA((2, 4, 15)),
            pltpu.SemaphoreType.DMA((2, 4, 15)),
        ],
        compiler_params=pltpu.CompilerParams(
            collective_id=0, has_side_effects=True, vmem_limit_bytes=48 * 1024 * 1024
        ),
        name="step",
    )(*args)


TURN = 256


def finish_kernel(
    codes,
    smooth,
    master,
    one,
    two,
    small,
    mine,
    weights_out,
    average_out,
    master_out,
    one_out,
    two_out,
    small_out,
    small_one_out,
    small_two_out,
    small_weights_out,
    small_average_out,
):
    step = pl.program_id(0)
    last = COLS // TURN

    def turn(width, first):
        cut = (slice(None), slice(None), pl.ds(first, width))
        new = decode_weight(codes[cut].astype(jnp.int32).reshape(SHARDS * ROWS, width).T)
        weights_out[pl.ds(0, width), :] = new.astype(jnp.bfloat16)
        average_out[pl.ds(0, width), :] = smooth[pl.ds(first, width), :] + (1.0 - decay_rate) * new

    @pl.when(step < last)
    def _():
        turn(TURN, pl.multiple_of(step * TURN, TURN))

    @pl.when(step == last)
    def _():
        turn(COLS - last * TURN, last * TURN)

    @pl.when(step == 0)
    def _():
        master_out[...] = master[...]
        one_out[...] = one[...]
        two_out[...] = two[...]
        small_out[...] = mine[0:1, 0:SEG]
        small_one_out[...] = mine[1:2, 0:SEG]
        small_two_out[...] = mine[2:3, 0:SEG]
        small_weights_out[...] = small[0:1, 0:SMALL].astype(jnp.bfloat16)
        small_average_out[...] = small[3:4, 0:SMALL]


def finish(codes, smooth, master, one, two, small, mine):
    def whole(*shape):
        return pl.BlockSpec(shape, lambda i: (0,) * len(shape))

    vmem = pl.BlockSpec(memory_space=pltpu.VMEM)
    f32, bf16 = jnp.float32, jnp.bfloat16
    rows = jax.ShapeDtypeStruct((MINE, ALL_COLS), f32)
    few = jax.ShapeDtypeStruct((1, SEG), f32)
    turned = pl.BlockSpec((TURN, SHARDS * ROWS), lambda i: (i, 0))
    return pl.pallas_call(
        finish_kernel,
        grid=(pl.cdiv(COLS, TURN),),
        in_specs=[vmem] * 7,
        out_specs=[turned, turned] + [whole(MINE, ALL_COLS)] * 3 + [whole(1, SEG)] * 3 + [whole(1, SMALL)] * 2,
        out_shape=(
            jax.ShapeDtypeStruct((COLS, SHARDS * ROWS), bf16),
            jax.ShapeDtypeStruct((COLS, SHARDS * ROWS), f32),
            rows,
            rows,
            rows,
            few,
            few,
            few,
            jax.ShapeDtypeStruct((1, SMALL), bf16),
            jax.ShapeDtypeStruct((1, SMALL), f32),
        ),
        compiler_params=pltpu.CompilerParams(vmem_limit_bytes=32 * 1024 * 1024),
        name="finish",
    )(codes, smooth, master, one, two, small, mine)


def shards(
    grads,
    small_grads,
    counts,
    step,
    master,
    moment_one,
    moment_two,
    average,
    small_master,
    small_one,
    small_two,
    small_average,
):
    new_master, new_one, new_two, small, mine, codes, smooth = communicate(
        counts,
        step,
        small_grads,
        small_master,
        small_one,
        small_two,
        small_average,
        grads.transpose(0, 2, 1),
        master,
        moment_one,
        moment_two,
        average,
    )
    (weights, averages, new_master, new_one, new_two, small_new, small_new_one, small_new_two, small_weights, small_averages) = finish(
        codes, smooth, new_master, new_one, new_two, small, mine
    )
    return (
        new_master,
        new_one,
        new_two,
        small_new,
        small_new_one,
        small_new_two,
        weights.T,
        small_weights.reshape(SMALL),
        averages.T,
        small_averages.reshape(SMALL),
    )


def solution(mesh):
    placed = (
        P("shard", None, "tensor"),
        P("shard", "tensor"),
        P("shard"),
        P(),
        P(("shard", "tensor"), None),
        P(("shard", "tensor"), None),
        P(("shard", "tensor"), None),
        P(("shard", "tensor"), None),
        P("tensor", "shard"),
        P("tensor", "shard"),
        P("tensor", "shard"),
        P("tensor", "shard"),
    )
    return jax.shard_map(
        shards,
        mesh=mesh,
        in_specs=placed,
        out_specs=(
            P(("shard", "tensor"), None),
            P(("shard", "tensor"), None),
            P(("shard", "tensor"), None),
            P("tensor", "shard"),
            P("tensor", "shard"),
            P("tensor", "shard"),
            P(None, "tensor"),
            P("tensor"),
            P(None, "tensor"),
            P("tensor"),
        ),
        check_vma=False,
    )
```

```python
import jax
import jax.numpy as jnp
import numpy as np
from jax import lax
from jax.experimental import pallas as pl
from jax.experimental.pallas import tpu as pltpu
from jax.sharding import PartitionSpec as P

learn_rate = 0.002
beta_one = 0.9
beta_two = 0.999
adam_eps = 1e-08
weight_decay = 0.1
clip_norm = 1.0
decay_rate = 0.99

MESH = pl.DeviceIdType.MESH
RING = 4
SHARDS = RING * RING
TENSORS = 8
ROWS = 56
MINE = 7
COLS = 2080
ALL_COLS = COLS * TENSORS
SMALL = 368
SEG = 23
LANES = 384
PARTS = ((0, 512), (1536, 544), (512, 512), (1024, 512))
TOP = 32700.0
SUM_MAX = 2.0
AVERAGE_MAX = 0.02
WEIGHT_UNIT = 2.0**-33


def encode(x, most):
    scaled = jnp.abs(x) * (TOP**4 / most) + 1e-20
    root = (lax.rsqrt(lax.rsqrt(scaled)) + 0.5).astype(jnp.int32)
    return jnp.where(x < 0.0, -root, root).astype(jnp.int16)


def decode(code, most):
    root = code.astype(jnp.int32).astype(jnp.float32)
    return (root * root) * (root * jnp.abs(root)) * (most / TOP**4)


def encode_weight(x):
    units = jnp.minimum(jnp.abs(x) * (1.0 / WEIGHT_UNIT), 2147483520.0)
    whole = units.astype(jnp.int32)
    shift = jnp.zeros_like(whole)
    for bits in (16, 8, 4, 2, 1):
        shift = shift + jnp.where((whole >> shift) >= (1 << (bits + 10)), bits, 0)
    kept = whole >> shift
    cut = jnp.logical_or((kept << shift) != whole, whole.astype(jnp.float32) != units)
    code = ((shift << 10) + kept) | jnp.where(cut, 1, 0)
    return jnp.where(x < 0.0, -code, code).astype(jnp.int16)


def decode_weight(code):
    code = code.astype(jnp.int32)
    size = jnp.abs(code)
    shift = jnp.maximum((size >> 10) - 1, 0)
    value = ((size - (shift << 10)) << shift).astype(jnp.float32)
    return jnp.where(code < 0, -WEIGHT_UNIT, WEIGHT_UNIT) * value


def adam(param, first, second, gradient, bias_one, bias_two, decay):
    first_new = beta_one * first + (1.0 - beta_one) * gradient
    second_new = beta_two * second + (1.0 - beta_two) * gradient * gradient
    ratio = first_new / bias_one / (jnp.sqrt(second_new / bias_two) + adam_eps)
    return param - learn_rate * (ratio + decay * param), first_new, second_new


def bias(time, beta):
    total = jnp.float32(0.0)
    for bit in range(10):
        term = ((time >> bit) & 1).astype(jnp.float32) * (1.0 - float(np.float32(beta)) ** (1 << bit))
        total = total + term - total * term
    return total


def place(s, shape, along):
    own = lax.broadcasted_iota(jnp.int32, shape, along)
    every = lax.broadcasted_iota(jnp.int32, shape, 1 - along)
    return jnp.where(jnp.logical_and(every == own + SEG * s, own < SEG), 1.0, 0.0)


def exact_dot(a, b):
    return jnp.dot(a, b, precision=lax.Precision.HIGHEST, preferred_element_type=jnp.float32)


def wrap(position, shift, size):
    return lax.rem(position + (shift + size), size)


def step_kernel(
    counts,
    step,
    small_grads,
    small_master,
    small_one,
    small_two,
    small_average,
    grads_hbm,
    master_hbm,
    one_hbm,
    two_hbm,
    average_hbm,
    om,
    o1,
    o2,
    small_out,
    mine_out,
    wall,
    smooth_out,
    gv,
    loc,
    pm,
    p1,
    p2,
    pa,
    big_send,
    big_recv,
    kept,
    mid_send,
    mid_recv,
    total,
    chunk_send,
    chunk_recv,
    wchunk_send,
    wchunk_recv,
    achunk_send,
    achunk_recv,
    aall,
    norm_send,
    norm_t,
    norm_s,
    small_state,
    small_in,
    small_send,
    small_y,
    small_z,
    load_sem,
    rs_send_sem,
    rs_recv_sem,
    t_send_sem,
    t_recv_sem,
    n_send_sem,
    n_recv_sem,
    r_send_sem,
    r_recv_sem,
    ag_send_sem,
    ag_recv_sem,
):
    s = lax.axis_index("shard")
    t = lax.axis_index("tensor")
    pos = (lax.div(s, RING), lax.rem(s, RING))
    core_sign = 1 - 2 * lax.rem(t, 2)

    def ring_device(axis, p):
        return (p * RING + pos[1], t) if axis == 0 else (pos[0] * RING + p, t)

    def shard_of(axis, p, k):
        return p * RING + k if axis == 0 else k * RING + p

    loads = [(average_hbm, pa)]
    for first, width in PARTS:
        cut = (slice(None), pl.ds(first, width))
        loads.append((grads_hbm.at[cut], gv.at[cut]))
    loads += [(master_hbm, pm), (one_hbm, p1), (two_hbm, p2)]
    loads = [pltpu.make_async_copy(src, dst, load_sem.at[i]) for i, (src, dst) in enumerate(loads)]
    for load in loads:
        load.start()

    valid_one = jnp.minimum(jnp.maximum(counts[0], 0), 1).astype(jnp.float32)
    valid_two = jnp.minimum(jnp.maximum(counts[0] - 1, 0), 1).astype(jnp.float32)
    small_state[...] = jnp.zeros((8, 128), jnp.float32)
    for i, ref in enumerate((small_master, small_one, small_two, small_average)):
        small_state[pl.ds(i + 1, 1), pl.ds(0, SEG)] = ref[...]
    small_in[...] = exact_dot(small_state[...], place(s, (128, LANES), 0))
    micro = small_grads[...].astype(jnp.float32)
    small_in[0:1, pl.ds(0, SMALL)] = valid_one * micro[0:1] + valid_two * micro[1:2]

    barrier = pltpu.get_barrier_semaphore()
    for d in range(1, SHARDS):
        pl.semaphore_signal(barrier, inc=1, device_id=(wrap(s, d, SHARDS), t), device_id_type=MESH)
    for d in range(1, TENSORS):
        pl.semaphore_signal(barrier, inc=1, device_id=(s, wrap(t, d, TENSORS)), device_id_type=MESH)
    pl.semaphore_wait(barrier, SHARDS - 1 + TENSORS - 1)

    pending = []

    def send(src, dst, send_sem, recv_sem, device):
        copy = pltpu.make_async_remote_copy(
            src_ref=src, dst_ref=dst, send_sem=send_sem, recv_sem=recv_sem, device_id=device, device_id_type=MESH
        )
        copy.start()
        pending.append(copy)
        return copy

    def ring_share(kind, axis, src, dst):
        return [
            send(
                src,
                dst.at[d - 1],
                r_send_sem.at[kind, d - 1],
                r_recv_sem.at[kind, d - 1],
                ring_device(axis, wrap(pos[axis], d, RING)),
            )
            for d in range(1, RING)
        ]

    def exchange(kind, src, dst):
        copies = []
        for d in range(1, TENSORS):
            to = wrap(t, d, TENSORS)
            copies.append(
                send(src.at[to], dst.at[t], t_send_sem.at[kind, d], t_recv_sem.at[kind, d], (s, to))
            )
        return copies

    loads[0].wait()
    half = ALL_COLS // 2
    for h in range(2):
        codes = pa[:, pl.ds(half * h, half)]
        for j in range(4):
            achunk_send[4 * h + j] = encode(codes[:, COLS * j : COLS * (j + 1)], AVERAGE_MAX)
    achunk_recv[t] = achunk_send[t]
    achunk_copies = exchange(3, achunk_send, achunk_recv)

    small_copies = ring_share(0, 0, small_in, small_y)

    def turn(q, tile):
        first, width = PARTS[q]
        cut = pl.ds(pl.multiple_of(tile * 128, 128), 128)
        a = gv[0, pl.ds(first, width), cut].astype(jnp.float32)
        b = gv[1, pl.ds(first, width), cut].astype(jnp.float32)
        loc[q][cut, :] = (valid_one * a + valid_two * b).T

    def local(shard, q):
        return loc[q][pl.ds(pl.multiple_of(shard * ROWS, 8), ROWS), :]

    axes = ((0, 1), (0, 1), (1, 0), (1, 0))
    signs = (core_sign, -core_sign, core_sign, -core_sign)
    order = [[wrap(pos[axes[q][1]], k, RING) for k in (2, signs[q], -signs[q], 0)] for q in range(4)]
    arrays = (wall, aall)

    def gather_send(x, q, shard, index, axis, sign):
        first, width = PARTS[q]
        ref = arrays[x].at[shard, :, pl.ds(first, width)]
        send(
            ref,
            ref,
            ag_send_sem.at[x, q, index],
            ag_recv_sem.at[x, q, index],
            ring_device(axis, wrap(pos[axis], sign, RING)),
        )

    def gather_wait(x, q, shard, index):
        first, width = PARTS[q]
        ref = arrays[x].at[shard, :, pl.ds(first, width)]
        pltpu.make_async_remote_copy(
            src_ref=ref,
            dst_ref=ref,
            send_sem=ag_send_sem.at[x, q, index],
            recv_sem=ag_recv_sem.at[x, q, index],
            device_id=ring_device(0, wrap(pos[0], 1, RING)),
            device_id_type=MESH,
        ).wait_recv()

    def outer(x, q, j, shard):
        axis, sign = axes[q][0], signs[q]
        gather_send(x, q, shard, 3 + 3 * j, axis, sign)
        gather_send(x, q, shard, 4 + 3 * j, axis, -sign)

    def source(q, shift, shift_outer):
        axis, other = axes[q]
        return shard_of(axis, wrap(pos[axis], shift_outer, RING), wrap(pos[other], shift, RING))

    def relay(x, q, j, shift):
        axis, sign = axes[q][0], signs[q]
        shard = source(q, shift, -sign)
        gather_wait(x, q, shard, 3 + 3 * j)
        gather_send(x, q, shard, 5 + 3 * j, axis, sign)

    def gather_first(x, q):
        other, sign = axes[q][1], signs[q]
        gather_send(x, q, s, 0, other, sign)
        gather_send(x, q, s, 1, other, -sign)
        outer(x, q, 0, s)

    def gather_second(x, q):
        other, sign = axes[q][1], signs[q]
        shard = source(q, -sign, 0)
        gather_wait(x, q, shard, 0)
        gather_send(x, q, shard, 2, other, sign)
        outer(x, q, 1, shard)
        relay(x, q, 0, 0)
        shard = source(q, sign, 0)
        gather_wait(x, q, shard, 1)
        outer(x, q, 2, shard)

    def gather_third(x, q):
        relay(x, q, 1, -signs[q])

    def gather_fourth(x, q):
        sign = signs[q]
        shard = source(q, 2, 0)
        gather_wait(x, q, shard, 2)
        outer(x, q, 3, shard)
        relay(x, q, 2, sign)

    def gather_fifth(x, q):
        relay(x, q, 3, 2)

    def gather_end(x, q):
        sign = signs[q]
        for j, shift in enumerate((0, -sign, sign, 2)):
            gather_wait(x, q, source(q, shift, sign), 4 + 3 * j)
            gather_wait(x, q, source(q, shift, 2), 5 + 3 * j)

    def turn_average(q):
        first, width = PARTS[q]
        for c in range(0, width, 128):
            some = min(128, width - c)
            codes = aall[:, :, pl.ds(first + c, some)].astype(jnp.int32).reshape(SHARDS * ROWS, some)
            smooth_out[pl.ds(first + c, some), :] = decay_rate * decode(codes.T, AVERAGE_MAX)

    early = [[None] * 2 for _ in range(4)]
    far = lax.min(lax.div(7 * wrap(pos[0], 2, RING), 4), 4)
    for slot in range(2):
        for q in range(4):
            axis, sign = axes[q][0], signs[q]
            p = pos[axis]
            dest = wrap(p, 2, RING) if slot == 0 else wrap(p, sign, RING)
            if slot == 0:
                loads[q + 1].wait()
            some = (0, 7) if axis == 1 else (0, 3) if slot == 0 else (3, 7)

            def tile(j, carry, q=q, axis=axis):
                turn(q, wrap(far, j, 7) if axis == 0 else j)
                return carry

            if slot == 0 or axis == 0:
                lax.fori_loop(*some, tile, 0)

            def fill(k, carry, q=q, axis=axis, dest=dest, slot=slot):
                big_send[q][slot, k] = encode(local(shard_of(axis, dest, k), q), SUM_MAX)
                return carry

            lax.fori_loop(0, RING, fill, 0)
            to = wrap(p, -sign, RING) if slot == 0 else dest
            early[q][slot] = send(
                big_send[q].at[slot],
                big_recv[q].at[slot],
                rs_send_sem.at[q, slot],
                rs_recv_sem.at[q, slot],
                ring_device(axis, to),
            )
    relayed = [[None] * RING for _ in range(4)]
    for q in range(4):
        early[q][0].wait_recv()
    for i in range(RING):
        for q in range(4):
            axis, sign = axes[q][0], signs[q]
            dest = wrap(pos[axis], -sign, RING)
            k = order[q][i]
            came = decode(big_recv[q][0, k], SUM_MAX)
            big_send[q][2, k] = encode(local(shard_of(axis, dest, k), q) + came, 2 * SUM_MAX)
            relayed[q][i] = send(
                big_send[q].at[2, k],
                big_recv[q].at[2, k],
                rs_send_sem.at[q, 2 + i],
                rs_recv_sem.at[q, 2 + i],
                ring_device(axis, dest),
            )
    for copy in small_copies:
        copy.wait_recv()
    small_send[...] = small_in[...] + small_y[0] + small_y[1] + small_y[2]
    small_copies = ring_share(1, 1, small_send, small_z)
    for q in range(4):
        early[q][1].wait_recv()
    for copy in achunk_copies:
        copy.wait_recv()
    aall[s] = jnp.concatenate([achunk_recv[j].astype(jnp.int32) for j in range(TENSORS)], axis=0).astype(jnp.int16)

    later = [[None] * 3 for _ in range(4)]
    for i in range(RING):
        for q in range(4):
            (axis, other), sign = axes[q], signs[q]
            k = order[q][i]
            relayed[q][i].wait_recv()
            piece = (
                local(shard_of(axis, pos[axis], k), q)
                + decode(big_recv[q][1, k], SUM_MAX)
                + decode(big_recv[q][2, k], 2 * SUM_MAX)
            )
            if i >= 2:
                kept[q][i - 2] = piece
                continue
            mid_send[q][i] = encode(piece, 4 * SUM_MAX)
            to = wrap(pos[other], -sign if i == 0 else sign, RING)
            later[q][i] = send(
                mid_send[q].at[i],
                mid_recv[q].at[i],
                rs_send_sem.at[q, 6 + i],
                rs_recv_sem.at[q, 6 + i],
                ring_device(other, to),
            )
    for q in range(4):
        other, sign = axes[q][1], signs[q]
        later[q][0].wait_recv()
        mid_send[q][2] = encode(kept[q][0] + decode(mid_recv[q][0], 4 * SUM_MAX), 8 * SUM_MAX)
        later[q][2] = send(
            mid_send[q].at[2],
            mid_recv[q].at[2],
            rs_send_sem.at[q, 8],
            rs_recv_sem.at[q, 8],
            ring_device(other, wrap(pos[other], -sign, RING)),
        )
    for q in range(4):
        gather_first(1, q)
    for copy in small_copies:
        copy.wait_recv()
    small_all = small_send[...] + small_z[0] + small_z[1] + small_z[2]
    small_sum = small_all[0:1]
    squares = jnp.sum(small_sum * small_sum) * (1.0 / SHARDS)
    for q in range(4):
        first, width = PARTS[q]
        later[q][1].wait_recv()
        later[q][2].wait_recv()
        piece = kept[q][1] + decode(mid_recv[q][1], 4 * SUM_MAX) + decode(mid_recv[q][2], 8 * SUM_MAX)
        total[:, pl.ds(first, width)] = piece
        squares = squares + jnp.sum(piece * piece)

    norm_send[0] = jnp.full((8, 128), squares, jnp.float32)
    norm_copies = []
    for d in range(1, TENSORS):
        norm_copies.append(
            send(
                norm_send.at[0],
                norm_t.at[d - 1],
                t_send_sem.at[0, d],
                t_recv_sem.at[0, d],
                (s, wrap(t, d, TENSORS)),
            )
        )
    for j in range(TENSORS):
        chunk_send[j] = encode(total[pl.ds(MINE * j, MINE), :], 16 * SUM_MAX)
    chunk_recv[t] = chunk_send[t]

    chunk_copies = exchange(1, chunk_send, chunk_recv)
    for copy in norm_copies:
        copy.wait_recv()
    norm = norm_send[0]
    for d in range(TENSORS - 1):
        norm = norm + norm_t[d]
    norm_send[1] = norm
    norm_copies = []
    for d in range(1, SHARDS):
        to = wrap(s, d, SHARDS)
        norm_copies.append(
            send(norm_send.at[1], norm_s.at[s], n_send_sem.at[d], n_recv_sem.at[d], (to, t))
        )
    norm_s[s] = norm
    for q in range(4):
        gather_second(1, q)
    for copy in norm_copies:
        copy.wait_recv()
    norm = norm_s[0]
    for d in range(1, SHARDS):
        norm = norm + norm_s[d]
    norm = jnp.sqrt(norm)
    factor = jnp.minimum(1.0, clip_norm / (norm + 1e-06))[0:1, 0:1]

    bias_one, bias_two = bias(step[0], beta_one), bias(step[0], beta_two)
    for load in loads[5:]:
        load.wait()
    for copy in chunk_copies:
        copy.wait_recv()
    for h in range(2):
        cols = pl.ds(half * h, half)
        summed = jnp.concatenate([decode(chunk_recv[4 * h + j], 16 * SUM_MAX) for j in range(4)], axis=1)
        new, one, two = adam(pm[:, cols], p1[:, cols], p2[:, cols], summed * factor, bias_one, bias_two, weight_decay)
        om[:, cols] = new
        o1[:, cols] = one
        o2[:, cols] = two
        for j in range(4):
            wchunk_send[4 * h + j] = encode_weight(new[:, COLS * j : COLS * (j + 1)])
    wchunk_recv[t] = wchunk_send[t]
    wchunk_copies = exchange(2, wchunk_send, wchunk_recv)
    for q in range(4):
        gather_third(1, q)

    new, one, two = adam(
        small_all[1:2], small_all[2:3], small_all[3:4], small_sum * factor, bias_one, bias_two, 0.0
    )
    smooth = decay_rate * small_all[4:5] + (1.0 - decay_rate) * new
    small_out[0:1] = new
    small_out[1:2] = one
    small_out[2:3] = two
    small_out[3:4] = smooth
    small_out[4:8] = jnp.zeros((4, LANES), jnp.float32)
    mine_out[...] = exact_dot(small_out[...], place(s, (LANES, 128), 1))

    for q in range(4):
        gather_fourth(1, q)
    for copy in wchunk_copies:
        copy.wait_recv()
    wall[s] = jnp.concatenate([wchunk_recv[j].astype(jnp.int32) for j in range(TENSORS)], axis=0).astype(jnp.int16)
    for q in range(4):
        gather_first(0, q)
    for q in range(4):
        gather_fifth(1, q)
    for q in range(4):
        gather_second(0, q)
    for q in range(4):
        gather_end(1, q)
    for q in range(4):
        gather_third(0, q)
    for q in range(4):
        gather_fourth(0, q)
    for q in range(4):
        gather_fifth(0, q)
    for i in range(4):
        turn_average(i)
    for q in range(4):
        gather_end(0, q)
    for copy in pending:
        copy.wait_send()


def communicate(*args):
    hbm = pl.BlockSpec(memory_space=pl.ANY)
    vmem = pl.BlockSpec(memory_space=pltpu.VMEM)
    smem = pl.BlockSpec(memory_space=pltpu.SMEM)
    f32, bf16, i16 = jnp.float32, jnp.bfloat16, jnp.int16
    widths = [w for _, w in PARTS]
    chunk = (TENSORS, MINE, COLS)
    return pl.pallas_call(
        step_kernel,
        out_shape=(
            *[pltpu.VMEM((MINE, ALL_COLS), f32)] * 3,
            pltpu.VMEM((8, LANES), f32),
            pltpu.VMEM((8, 128), f32),
            pltpu.VMEM((SHARDS, ROWS, COLS), i16),
            pltpu.VMEM((COLS, SHARDS * ROWS), f32),
        ),
        in_specs=[smem] * 2 + [vmem] * 5 + [hbm] * 5,
        out_specs=(vmem,) * 7,
        scratch_shapes=[
            pltpu.VMEM((2, COLS, SHARDS * ROWS), bf16),
            [pltpu.VMEM((SHARDS * ROWS, w), f32) for w in widths],
            *[pltpu.VMEM((MINE, ALL_COLS), f32)] * 4,
            [pltpu.VMEM((3, RING, ROWS, w), i16) for w in widths],
            [pltpu.VMEM((3, RING, ROWS, w), i16) for w in widths],
            [pltpu.VMEM((2, ROWS, w), f32) for w in widths],
            [pltpu.VMEM((3, ROWS, w), i16) for w in widths],
            [pltpu.VMEM((3, ROWS, w), i16) for w in widths],
            pltpu.VMEM((ROWS, COLS), f32),
            pltpu.VMEM(chunk, i16),
            pltpu.VMEM(chunk, i16),
            pltpu.VMEM(chunk, i16),
            pltpu.VMEM(chunk, i16),
            pltpu.VMEM(chunk, i16),
            pltpu.VMEM(chunk, i16),
            pltpu.VMEM((SHARDS, ROWS, COLS), i16),
            pltpu.VMEM((2, 8, 128), f32),
            pltpu.VMEM((TENSORS - 1, 8, 128), f32),
            pltpu.VMEM((SHARDS, 8, 128), f32),
            pltpu.VMEM((8, 128), f32),
            pltpu.VMEM((8, LANES), f32),
            pltpu.VMEM((8, LANES), f32),
            pltpu.VMEM((RING - 1, 8, LANES), f32),
            pltpu.VMEM((RING - 1, 8, LANES), f32),
            pltpu.SemaphoreType.DMA((8,)),
            pltpu.SemaphoreType.DMA((4, 9)),
            pltpu.SemaphoreType.DMA((4, 9)),
            pltpu.SemaphoreType.DMA((4, TENSORS)),
            pltpu.SemaphoreType.DMA((4, TENSORS)),
            pltpu.SemaphoreType.DMA((SHARDS,)),
            pltpu.SemaphoreType.DMA((SHARDS,)),
            pltpu.SemaphoreType.DMA((2, RING - 1)),
            pltpu.SemaphoreType.DMA((2, RING - 1)),
            pltpu.SemaphoreType.DMA((2, 4, 15)),
            pltpu.SemaphoreType.DMA((2, 4, 15)),
        ],
        compiler_params=pltpu.CompilerParams(
            collective_id=0, has_side_effects=True, vmem_limit_bytes=48 * 1024 * 1024
        ),
        name="step",
    )(*args)


TURN = 512


def finish_kernel(
    codes,
    smooth,
    master,
    one,
    two,
    small,
    mine,
    weights_out,
    average_out,
    master_out,
    one_out,
    two_out,
    small_out,
    small_one_out,
    small_two_out,
    small_weights_out,
    small_average_out,
):
    step = pl.program_id(0)
    last = COLS // TURN

    def turn(width, first):
        cut = (slice(None), slice(None), pl.ds(first, width))
        new = decode_weight(codes[cut].astype(jnp.int32).reshape(SHARDS * ROWS, width).T)
        weights_out[pl.ds(0, width), :] = new.astype(jnp.bfloat16)
        average_out[pl.ds(0, width), :] = smooth[pl.ds(first, width), :] + (1.0 - decay_rate) * new

    @pl.when(step < last)
    def _():
        turn(TURN, pl.multiple_of(step * TURN, TURN))

    @pl.when(step == last)
    def _():
        turn(COLS - last * TURN, last * TURN)

    @pl.when(step == 0)
    def _():
        master_out[...] = master[...]
        one_out[...] = one[...]
        two_out[...] = two[...]
        small_out[...] = mine[0:1, 0:SEG]
        small_one_out[...] = mine[1:2, 0:SEG]
        small_two_out[...] = mine[2:3, 0:SEG]
        small_weights_out[...] = small[0, 0:SMALL].astype(jnp.bfloat16)
        small_average_out[...] = small[3, 0:SMALL]


def finish(codes, smooth, master, one, two, small, mine):
    def whole(*shape):
        return pl.BlockSpec(shape, lambda i: (0,) * len(shape))

    vmem = pl.BlockSpec(memory_space=pltpu.VMEM)
    f32, bf16 = jnp.float32, jnp.bfloat16
    rows = jax.ShapeDtypeStruct((MINE, ALL_COLS), f32)
    few = jax.ShapeDtypeStruct((1, SEG), f32)
    turned = pl.BlockSpec((TURN, SHARDS * ROWS), lambda i: (i, 0))
    return pl.pallas_call(
        finish_kernel,
        grid=(pl.cdiv(COLS, TURN),),
        in_specs=[vmem] * 7,
        out_specs=[turned, turned] + [whole(MINE, ALL_COLS)] * 3 + [whole(1, SEG)] * 3 + [whole(SMALL)] * 2,
        out_shape=(
            jax.ShapeDtypeStruct((COLS, SHARDS * ROWS), bf16),
            jax.ShapeDtypeStruct((COLS, SHARDS * ROWS), f32),
            rows,
            rows,
            rows,
            few,
            few,
            few,
            jax.ShapeDtypeStruct((SMALL,), bf16),
            jax.ShapeDtypeStruct((SMALL,), f32),
        ),
        compiler_params=pltpu.CompilerParams(vmem_limit_bytes=32 * 1024 * 1024),
        name="finish",
    )(codes, smooth, master, one, two, small, mine)


def shards(
    grads,
    small_grads,
    counts,
    step,
    master,
    moment_one,
    moment_two,
    average,
    small_master,
    small_one,
    small_two,
    small_average,
):
    new_master, new_one, new_two, small, mine, codes, smooth = communicate(
        counts,
        step,
        small_grads,
        small_master,
        small_one,
        small_two,
        small_average,
        grads.transpose(0, 2, 1),
        master,
        moment_one,
        moment_two,
        average,
    )
    (weights, averages, new_master, new_one, new_two, small_new, small_new_one, small_new_two, small_weights, small_averages) = finish(
        codes, smooth, new_master, new_one, new_two, small, mine
    )
    return (
        new_master,
        new_one,
        new_two,
        small_new,
        small_new_one,
        small_new_two,
        weights.T,
        small_weights,
        averages.T,
        small_averages,
    )


def solution(mesh):
    placed = (
        P("shard", None, "tensor"),
        P("shard", "tensor"),
        P("shard"),
        P(),
        P(("shard", "tensor"), None),
        P(("shard", "tensor"), None),
        P(("shard", "tensor"), None),
        P(("shard", "tensor"), None),
        P("tensor", "shard"),
        P("tensor", "shard"),
        P("tensor", "shard"),
        P("tensor", "shard"),
    )
    return jax.shard_map(
        shards,
        mesh=mesh,
        in_specs=placed,
        out_specs=(
            P(("shard", "tensor"), None),
            P(("shard", "tensor"), None),
            P(("shard", "tensor"), None),
            P("tensor", "shard"),
            P("tensor", "shard"),
            P("tensor", "shard"),
            P(None, "tensor"),
            P("tensor"),
            P(None, "tensor"),
            P("tensor"),
        ),
        check_vma=False,
    )
```

```python
import jax
import jax.numpy as jnp
import numpy as np
from jax import lax
from jax.experimental import pallas as pl
from jax.experimental.pallas import tpu as pltpu
from jax.sharding import PartitionSpec as P

learn_rate = 0.002
beta_one = 0.9
beta_two = 0.999
adam_eps = 1e-08
weight_decay = 0.1
clip_norm = 1.0
decay_rate = 0.99

MESH = pl.DeviceIdType.MESH
RING = 4
SHARDS = RING * RING
TENSORS = 8
ROWS = 56
MINE = 7
COLS = 2080
ALL_COLS = COLS * TENSORS
SMALL = 368
SEG = 23
LANES = 384
PARTS = ((0, 512), (1536, 544), (512, 512), (1024, 512))
TOP = 32700.0
SUM_MAX = 2.0
AVERAGE_MAX = 0.02
WEIGHT_UNIT = 2.0**-33


def encode(x, most):
    scaled = jnp.abs(x) * (TOP**4 / most) + 1e-20
    root = (lax.rsqrt(lax.rsqrt(scaled)) + 0.5).astype(jnp.int32)
    return jnp.where(x < 0.0, -root, root).astype(jnp.int16)


def decode(code, most):
    root = code.astype(jnp.int32).astype(jnp.float32)
    return (root * root) * (root * jnp.abs(root)) * (most / TOP**4)


def encode_weight(x):
    units = jnp.minimum(jnp.abs(x) * (1.0 / WEIGHT_UNIT), 2147483520.0)
    whole = units.astype(jnp.int32)
    shift = jnp.zeros_like(whole)
    for bits in (16, 8, 4, 2, 1):
        shift = shift + jnp.where((whole >> shift) >= (1 << (bits + 10)), bits, 0)
    kept = whole >> shift
    cut = jnp.logical_or((kept << shift) != whole, whole.astype(jnp.float32) != units)
    code = ((shift << 10) + kept) | jnp.where(cut, 1, 0)
    return jnp.where(x < 0.0, -code, code).astype(jnp.int16)


def decode_weight(code):
    code = code.astype(jnp.int32)
    size = jnp.abs(code)
    shift = jnp.maximum((size >> 10) - 1, 0)
    value = ((size - (shift << 10)) << shift).astype(jnp.float32)
    return jnp.where(code < 0, -WEIGHT_UNIT, WEIGHT_UNIT) * value


def adam(param, first, second, gradient, bias_one, bias_two, decay):
    first_new = beta_one * first + (1.0 - beta_one) * gradient
    second_new = beta_two * second + (1.0 - beta_two) * gradient * gradient
    ratio = first_new / bias_one / (jnp.sqrt(second_new / bias_two) + adam_eps)
    return param - learn_rate * (ratio + decay * param), first_new, second_new


def bias(time, beta):
    total = jnp.float32(0.0)
    for bit in range(10):
        term = ((time >> bit) & 1).astype(jnp.float32) * (1.0 - float(np.float32(beta)) ** (1 << bit))
        total = total + term - total * term
    return total


def place(s, shape, along):
    own = lax.broadcasted_iota(jnp.int32, shape, along)
    every = lax.broadcasted_iota(jnp.int32, shape, 1 - along)
    return jnp.where(jnp.logical_and(every == own + SEG * s, own < SEG), 1.0, 0.0)


def exact_dot(a, b):
    return jnp.dot(a, b, precision=lax.Precision.HIGHEST, preferred_element_type=jnp.float32)


def wrap(position, shift, size):
    return lax.rem(position + (shift + size), size)


def step_kernel(
    counts,
    step,
    small_grads,
    small_master,
    small_one,
    small_two,
    small_average,
    grads_hbm,
    master_hbm,
    one_hbm,
    two_hbm,
    average_hbm,
    om,
    o1,
    o2,
    small_out,
    mine_out,
    wall,
    smooth_out,
    gv,
    loc,
    pm,
    p1,
    p2,
    pa,
    big_send,
    big_recv,
    kept,
    mid_send,
    mid_recv,
    total,
    chunk_send,
    chunk_recv,
    wchunk_send,
    wchunk_recv,
    achunk_send,
    achunk_recv,
    aall,
    norm_send,
    norm_t,
    norm_s,
    small_state,
    small_in,
    small_send,
    small_y,
    small_z,
    load_sem,
    rs_send_sem,
    rs_recv_sem,
    t_send_sem,
    t_recv_sem,
    n_send_sem,
    n_recv_sem,
    r_send_sem,
    r_recv_sem,
    ag_send_sem,
    ag_recv_sem,
):
    s = lax.axis_index("shard")
    t = lax.axis_index("tensor")
    pos = (lax.div(s, RING), lax.rem(s, RING))
    core_sign = 1 - 2 * lax.rem(t, 2)

    def ring_device(axis, p):
        return (p * RING + pos[1], t) if axis == 0 else (pos[0] * RING + p, t)

    def shard_of(axis, p, k):
        return p * RING + k if axis == 0 else k * RING + p

    barrier = pltpu.get_barrier_semaphore()
    for d in range(1, SHARDS):
        pl.semaphore_signal(barrier, inc=1, device_id=(wrap(s, d, SHARDS), t), device_id_type=MESH)
    for d in range(1, TENSORS):
        pl.semaphore_signal(barrier, inc=1, device_id=(s, wrap(t, d, TENSORS)), device_id_type=MESH)

    loads = [(average_hbm, pa)]
    for first, width in PARTS:
        cut = (slice(None), pl.ds(first, width))
        loads.append((grads_hbm.at[cut], gv.at[cut]))
    loads += [(master_hbm, pm), (one_hbm, p1), (two_hbm, p2)]
    loads = [pltpu.make_async_copy(src, dst, load_sem.at[i]) for i, (src, dst) in enumerate(loads)]
    for load in loads:
        load.start()

    valid_one = jnp.minimum(jnp.maximum(counts[0], 0), 1).astype(jnp.float32)
    valid_two = jnp.minimum(jnp.maximum(counts[0] - 1, 0), 1).astype(jnp.float32)
    small_state[...] = jnp.zeros((8, 128), jnp.float32)
    for i, ref in enumerate((small_master, small_one, small_two, small_average)):
        small_state[pl.ds(i + 1, 1), pl.ds(0, SEG)] = ref[...]
    small_in[...] = exact_dot(small_state[...], place(s, (128, LANES), 0))
    micro = small_grads[...].astype(jnp.float32)
    small_in[0:1, pl.ds(0, SMALL)] = valid_one * micro[0:1] + valid_two * micro[1:2]

    pending = []

    def send(src, dst, send_sem, recv_sem, device):
        copy = pltpu.make_async_remote_copy(
            src_ref=src, dst_ref=dst, send_sem=send_sem, recv_sem=recv_sem, device_id=device, device_id_type=MESH
        )
        copy.start()
        pending.append(copy)
        return copy

    def ring_share(kind, axis, src, dst):
        return [
            send(
                src,
                dst.at[d - 1],
                r_send_sem.at[kind, d - 1],
                r_recv_sem.at[kind, d - 1],
                ring_device(axis, wrap(pos[axis], d, RING)),
            )
            for d in range(1, RING)
        ]

    def exchange(kind, src, dst):
        copies = []
        for d in range(1, TENSORS):
            to = wrap(t, d, TENSORS)
            copies.append(
                send(src.at[to], dst.at[t], t_send_sem.at[kind, d], t_recv_sem.at[kind, d], (s, to))
            )
        return copies

    loads[0].wait()
    half = ALL_COLS // 2
    for h in range(2):
        codes = pa[:, pl.ds(half * h, half)]
        for j in range(4):
            achunk_send[4 * h + j] = encode(codes[:, COLS * j : COLS * (j + 1)], AVERAGE_MAX)
    achunk_recv[t] = achunk_send[t]


    def turn(q, tile):
        first, width = PARTS[q]
        cut = pl.ds(pl.multiple_of(tile * 128, 128), 128)
        a = gv[0, pl.ds(first, width), cut].astype(jnp.float32)
        b = gv[1, pl.ds(first, width), cut].astype(jnp.float32)
        loc[q][cut, :] = (valid_one * a + valid_two * b).T

    def local(shard, q):
        return loc[q][pl.ds(pl.multiple_of(shard * ROWS, 8), ROWS), :]

    axes = ((0, 1), (0, 1), (1, 0), (1, 0))
    signs = (core_sign, -core_sign, core_sign, -core_sign)
    order = [[wrap(pos[axes[q][1]], k, RING) for k in (2, signs[q], -signs[q], 0)] for q in range(4)]
    arrays = (wall, aall)

    def gather_send(x, q, shard, index, axis, sign):
        first, width = PARTS[q]
        ref = arrays[x].at[shard, :, pl.ds(first, width)]
        send(
            ref,
            ref,
            ag_send_sem.at[x, q, index],
            ag_recv_sem.at[x, q, index],
            ring_device(axis, wrap(pos[axis], sign, RING)),
        )

    def gather_wait(x, q, shard, index):
        first, width = PARTS[q]
        ref = arrays[x].at[shard, :, pl.ds(first, width)]
        pltpu.make_async_remote_copy(
            src_ref=ref,
            dst_ref=ref,
            send_sem=ag_send_sem.at[x, q, index],
            recv_sem=ag_recv_sem.at[x, q, index],
            device_id=ring_device(0, wrap(pos[0], 1, RING)),
            device_id_type=MESH,
        ).wait_recv()

    def outer(x, q, j, shard):
        axis, sign = axes[q][0], signs[q]
        gather_send(x, q, shard, 3 + 3 * j, axis, sign)
        gather_send(x, q, shard, 4 + 3 * j, axis, -sign)

    def source(q, shift, shift_outer):
        axis, other = axes[q]
        return shard_of(axis, wrap(pos[axis], shift_outer, RING), wrap(pos[other], shift, RING))

    def relay(x, q, j, shift):
        axis, sign = axes[q][0], signs[q]
        shard = source(q, shift, -sign)
        gather_wait(x, q, shard, 3 + 3 * j)
        gather_send(x, q, shard, 5 + 3 * j, axis, sign)

    def gather_first(x, q):
        other, sign = axes[q][1], signs[q]
        gather_send(x, q, s, 0, other, sign)
        gather_send(x, q, s, 1, other, -sign)
        outer(x, q, 0, s)

    def gather_second(x, q):
        other, sign = axes[q][1], signs[q]
        shard = source(q, -sign, 0)
        gather_wait(x, q, shard, 0)
        gather_send(x, q, shard, 2, other, sign)
        outer(x, q, 1, shard)
        relay(x, q, 0, 0)
        shard = source(q, sign, 0)
        gather_wait(x, q, shard, 1)
        outer(x, q, 2, shard)

    def gather_third(x, q):
        relay(x, q, 1, -signs[q])

    def gather_fourth(x, q):
        sign = signs[q]
        shard = source(q, 2, 0)
        gather_wait(x, q, shard, 2)
        outer(x, q, 3, shard)
        relay(x, q, 2, sign)

    def gather_fifth(x, q):
        relay(x, q, 3, 2)

    def gather_end(x, q):
        sign = signs[q]
        for j, shift in enumerate((0, -sign, sign, 2)):
            gather_wait(x, q, source(q, shift, sign), 4 + 3 * j)
            gather_wait(x, q, source(q, shift, 2), 5 + 3 * j)

    def turn_average(q):
        first, width = PARTS[q]
        for c in range(0, width, 128):
            some = min(128, width - c)
            codes = aall[:, :, pl.ds(first + c, some)].astype(jnp.int32).reshape(SHARDS * ROWS, some)
            smooth_out[pl.ds(first + c, some), :] = decay_rate * decode(codes.T, AVERAGE_MAX)

    early = [[None] * 2 for _ in range(4)]
    far = lax.min(lax.div(7 * wrap(pos[0], 2, RING), 4), 4)
    for slot in range(2):
        for q in range(4):
            axis, sign = axes[q][0], signs[q]
            p = pos[axis]
            dest = wrap(p, 2, RING) if slot == 0 else wrap(p, sign, RING)
            if slot == 0:
                loads[q + 1].wait()
            some = (0, 7) if axis == 1 else (0, 3) if slot == 0 else (3, 7)

            def tile(j, carry, q=q, axis=axis):
                turn(q, wrap(far, j, 7) if axis == 0 else j)
                return carry

            if slot == 0 or axis == 0:
                lax.fori_loop(*some, tile, 0)

            def fill(k, carry, q=q, axis=axis, dest=dest, slot=slot):
                big_send[q][slot, k] = encode(local(shard_of(axis, dest, k), q), SUM_MAX)
                return carry

            lax.fori_loop(0, RING, fill, 0)
            if slot == 0 and q == 0:
                pl.semaphore_wait(barrier, SHARDS - 1 + TENSORS - 1)
            to = wrap(p, -sign, RING) if slot == 0 else dest
            early[q][slot] = send(
                big_send[q].at[slot],
                big_recv[q].at[slot],
                rs_send_sem.at[q, slot],
                rs_recv_sem.at[q, slot],
                ring_device(axis, to),
            )
            if slot == 0 and q == 1:
                achunk_copies = exchange(3, achunk_send, achunk_recv)
                small_copies = ring_share(0, 0, small_in, small_y)
    relayed = [[None] * RING for _ in range(4)]
    for q in range(4):
        early[q][0].wait_recv()
    for i in range(RING):
        for q in range(4):
            axis, sign = axes[q][0], signs[q]
            dest = wrap(pos[axis], -sign, RING)
            k = order[q][i]
            came = decode(big_recv[q][0, k], SUM_MAX)
            big_send[q][2, k] = encode(local(shard_of(axis, dest, k), q) + came, 2 * SUM_MAX)
            relayed[q][i] = send(
                big_send[q].at[2, k],
                big_recv[q].at[2, k],
                rs_send_sem.at[q, 2 + i],
                rs_recv_sem.at[q, 2 + i],
                ring_device(axis, dest),
            )
    for copy in small_copies:
        copy.wait_recv()
    small_send[...] = small_in[...] + small_y[0] + small_y[1] + small_y[2]
    small_copies = ring_share(1, 1, small_send, small_z)
    for q in range(4):
        early[q][1].wait_recv()
    for copy in achunk_copies:
        copy.wait_recv()
    aall[s] = jnp.concatenate([achunk_recv[j].astype(jnp.int32) for j in range(TENSORS)], axis=0).astype(jnp.int16)

    later = [[None] * 3 for _ in range(4)]
    for i in range(RING):
        for q in range(4):
            (axis, other), sign = axes[q], signs[q]
            k = order[q][i]
            relayed[q][i].wait_recv()
            piece = (
                local(shard_of(axis, pos[axis], k), q)
                + decode(big_recv[q][1, k], SUM_MAX)
                + decode(big_recv[q][2, k], 2 * SUM_MAX)
            )
            if i >= 2:
                kept[q][i - 2] = piece
                continue
            mid_send[q][i] = encode(piece, 4 * SUM_MAX)
            to = wrap(pos[other], -sign if i == 0 else sign, RING)
            later[q][i] = send(
                mid_send[q].at[i],
                mid_recv[q].at[i],
                rs_send_sem.at[q, 6 + i],
                rs_recv_sem.at[q, 6 + i],
                ring_device(other, to),
            )
    for q in range(4):
        other, sign = axes[q][1], signs[q]
        later[q][0].wait_recv()
        mid_send[q][2] = encode(kept[q][0] + decode(mid_recv[q][0], 4 * SUM_MAX), 8 * SUM_MAX)
        later[q][2] = send(
            mid_send[q].at[2],
            mid_recv[q].at[2],
            rs_send_sem.at[q, 8],
            rs_recv_sem.at[q, 8],
            ring_device(other, wrap(pos[other], -sign, RING)),
        )
    for q in range(4):
        gather_first(1, q)
    for copy in small_copies:
        copy.wait_recv()
    small_all = small_send[...] + small_z[0] + small_z[1] + small_z[2]
    small_sum = small_all[0:1]
    squares = jnp.sum(small_sum * small_sum) * (1.0 / SHARDS)
    for q in range(4):
        first, width = PARTS[q]
        later[q][1].wait_recv()
        later[q][2].wait_recv()
        piece = kept[q][1] + decode(mid_recv[q][1], 4 * SUM_MAX) + decode(mid_recv[q][2], 8 * SUM_MAX)
        total[:, pl.ds(first, width)] = piece
        squares = squares + jnp.sum(piece * piece)

    norm_send[0] = jnp.full((8, 128), squares, jnp.float32)
    norm_copies = []
    for d in range(1, TENSORS):
        norm_copies.append(
            send(
                norm_send.at[0],
                norm_t.at[d - 1],
                t_send_sem.at[0, d],
                t_recv_sem.at[0, d],
                (s, wrap(t, d, TENSORS)),
            )
        )
    for j in range(TENSORS):
        chunk_send[j] = encode(total[pl.ds(MINE * j, MINE), :], 16 * SUM_MAX)
    chunk_recv[t] = chunk_send[t]

    chunk_copies = exchange(1, chunk_send, chunk_recv)
    for copy in norm_copies:
        copy.wait_recv()
    norm = norm_send[0]
    for d in range(TENSORS - 1):
        norm = norm + norm_t[d]
    norm_send[1] = norm
    norm_copies = []
    for d in range(1, SHARDS):
        to = wrap(s, d, SHARDS)
        norm_copies.append(
            send(norm_send.at[1], norm_s.at[s], n_send_sem.at[d], n_recv_sem.at[d], (to, t))
        )
    norm_s[s] = norm
    for q in range(4):
        gather_second(1, q)
    for copy in norm_copies:
        copy.wait_recv()
    norm = norm_s[0]
    for d in range(1, SHARDS):
        norm = norm + norm_s[d]
    norm = jnp.sqrt(norm)
    factor = jnp.minimum(1.0, clip_norm / (norm + 1e-06))[0:1, 0:1]

    bias_one, bias_two = bias(step[0], beta_one), bias(step[0], beta_two)
    for load in loads[5:]:
        load.wait()
    for copy in chunk_copies:
        copy.wait_recv()
    for h in range(2):
        cols = pl.ds(half * h, half)
        summed = jnp.concatenate([decode(chunk_recv[4 * h + j], 16 * SUM_MAX) for j in range(4)], axis=1)
        new, one, two = adam(pm[:, cols], p1[:, cols], p2[:, cols], summed * factor, bias_one, bias_two, weight_decay)
        om[:, cols] = new
        o1[:, cols] = one
        o2[:, cols] = two
        for j in range(4):
            wchunk_send[4 * h + j] = encode_weight(new[:, COLS * j : COLS * (j + 1)])
    wchunk_recv[t] = wchunk_send[t]
    wchunk_copies = exchange(2, wchunk_send, wchunk_recv)
    for q in range(4):
        gather_third(1, q)

    new, one, two = adam(
        small_all[1:2], small_all[2:3], small_all[3:4], small_sum * factor, bias_one, bias_two, 0.0
    )
    smooth = decay_rate * small_all[4:5] + (1.0 - decay_rate) * new
    small_out[0:1] = new
    small_out[1:2] = one
    small_out[2:3] = two
    small_out[3:4] = smooth
    small_out[4:8] = jnp.zeros((4, LANES), jnp.float32)
    mine_out[...] = exact_dot(small_out[...], place(s, (LANES, 128), 1))

    for q in range(4):
        gather_fourth(1, q)
    for copy in wchunk_copies:
        copy.wait_recv()
    wall[s] = jnp.concatenate([wchunk_recv[j].astype(jnp.int32) for j in range(TENSORS)], axis=0).astype(jnp.int16)
    for q in range(4):
        gather_first(0, q)
    for q in range(4):
        gather_fifth(1, q)
    for q in range(4):
        gather_second(0, q)
    for q in range(4):
        gather_end(1, q)
    for q in range(4):
        gather_third(0, q)
    for q in range(4):
        gather_fourth(0, q)
    for q in range(4):
        gather_fifth(0, q)
    for i in range(4):
        turn_average(i)
    for q in range(4):
        gather_end(0, q)
    for copy in pending:
        copy.wait_send()


def communicate(*args):
    hbm = pl.BlockSpec(memory_space=pl.ANY)
    vmem = pl.BlockSpec(memory_space=pltpu.VMEM)
    smem = pl.BlockSpec(memory_space=pltpu.SMEM)
    f32, bf16, i16 = jnp.float32, jnp.bfloat16, jnp.int16
    widths = [w for _, w in PARTS]
    chunk = (TENSORS, MINE, COLS)
    return pl.pallas_call(
        step_kernel,
        out_shape=(
            *[pltpu.VMEM((MINE, ALL_COLS), f32)] * 3,
            pltpu.VMEM((8, LANES), f32),
            pltpu.VMEM((8, 128), f32),
            pltpu.VMEM((SHARDS, ROWS, COLS), i16),
            pltpu.VMEM((COLS, SHARDS * ROWS), f32),
        ),
        in_specs=[smem] * 2 + [vmem] * 5 + [hbm] * 5,
        out_specs=(vmem,) * 7,
        scratch_shapes=[
            pltpu.VMEM((2, COLS, SHARDS * ROWS), bf16),
            [pltpu.VMEM((SHARDS * ROWS, w), f32) for w in widths],
            *[pltpu.VMEM((MINE, ALL_COLS), f32)] * 4,
            [pltpu.VMEM((3, RING, ROWS, w), i16) for w in widths],
            [pltpu.VMEM((3, RING, ROWS, w), i16) for w in widths],
            [pltpu.VMEM((2, ROWS, w), f32) for w in widths],
            [pltpu.VMEM((3, ROWS, w), i16) for w in widths],
            [pltpu.VMEM((3, ROWS, w), i16) for w in widths],
            pltpu.VMEM((ROWS, COLS), f32),
            pltpu.VMEM(chunk, i16),
            pltpu.VMEM(chunk, i16),
            pltpu.VMEM(chunk, i16),
            pltpu.VMEM(chunk, i16),
            pltpu.VMEM(chunk, i16),
            pltpu.VMEM(chunk, i16),
            pltpu.VMEM((SHARDS, ROWS, COLS), i16),
            pltpu.VMEM((2, 8, 128), f32),
            pltpu.VMEM((TENSORS - 1, 8, 128), f32),
            pltpu.VMEM((SHARDS, 8, 128), f32),
            pltpu.VMEM((8, 128), f32),
            pltpu.VMEM((8, LANES), f32),
            pltpu.VMEM((8, LANES), f32),
            pltpu.VMEM((RING - 1, 8, LANES), f32),
            pltpu.VMEM((RING - 1, 8, LANES), f32),
            pltpu.SemaphoreType.DMA((8,)),
            pltpu.SemaphoreType.DMA((4, 9)),
            pltpu.SemaphoreType.DMA((4, 9)),
            pltpu.SemaphoreType.DMA((4, TENSORS)),
            pltpu.SemaphoreType.DMA((4, TENSORS)),
            pltpu.SemaphoreType.DMA((SHARDS,)),
            pltpu.SemaphoreType.DMA((SHARDS,)),
            pltpu.SemaphoreType.DMA((2, RING - 1)),
            pltpu.SemaphoreType.DMA((2, RING - 1)),
            pltpu.SemaphoreType.DMA((2, 4, 15)),
            pltpu.SemaphoreType.DMA((2, 4, 15)),
        ],
        compiler_params=pltpu.CompilerParams(
            collective_id=0, has_side_effects=True, vmem_limit_bytes=48 * 1024 * 1024
        ),
        name="step",
    )(*args)


TURN = 512


def finish_kernel(
    codes,
    smooth,
    master,
    one,
    two,
    small,
    mine,
    weights_out,
    average_out,
    master_out,
    one_out,
    two_out,
    small_out,
    small_one_out,
    small_two_out,
    small_weights_out,
    small_average_out,
):
    step = pl.program_id(0)
    last = COLS // TURN

    def turn(width, first):
        cut = (slice(None), slice(None), pl.ds(first, width))
        new = decode_weight(codes[cut].astype(jnp.int32).reshape(SHARDS * ROWS, width).T)
        weights_out[pl.ds(0, width), :] = new.astype(jnp.bfloat16)
        average_out[pl.ds(0, width), :] = smooth[pl.ds(first, width), :] + (1.0 - decay_rate) * new

    @pl.when(step < last)
    def _():
        turn(TURN, pl.multiple_of(step * TURN, TURN))

    @pl.when(step == last)
    def _():
        turn(COLS - last * TURN, last * TURN)

    @pl.when(step == 0)
    def _():
        master_out[...] = master[...]
        one_out[...] = one[...]
        two_out[...] = two[...]
        small_out[...] = mine[0:1, 0:SEG]
        small_one_out[...] = mine[1:2, 0:SEG]
        small_two_out[...] = mine[2:3, 0:SEG]
        small_weights_out[...] = small[0, 0:SMALL].astype(jnp.bfloat16)
        small_average_out[...] = small[3, 0:SMALL]


def finish(codes, smooth, master, one, two, small, mine):
    def whole(*shape):
        return pl.BlockSpec(shape, lambda i: (0,) * len(shape))

    vmem = pl.BlockSpec(memory_space=pltpu.VMEM)
    f32, bf16 = jnp.float32, jnp.bfloat16
    rows = jax.ShapeDtypeStruct((MINE, ALL_COLS), f32)
    few = jax.ShapeDtypeStruct((1, SEG), f32)
    turned = pl.BlockSpec((TURN, SHARDS * ROWS), lambda i: (i, 0))
    return pl.pallas_call(
        finish_kernel,
        grid=(pl.cdiv(COLS, TURN),),
        in_specs=[vmem] * 7,
        out_specs=[turned, turned] + [whole(MINE, ALL_COLS)] * 3 + [whole(1, SEG)] * 3 + [whole(SMALL)] * 2,
        out_shape=(
            jax.ShapeDtypeStruct((COLS, SHARDS * ROWS), bf16),
            jax.ShapeDtypeStruct((COLS, SHARDS * ROWS), f32),
            rows,
            rows,
            rows,
            few,
            few,
            few,
            jax.ShapeDtypeStruct((SMALL,), bf16),
            jax.ShapeDtypeStruct((SMALL,), f32),
        ),
        compiler_params=pltpu.CompilerParams(vmem_limit_bytes=32 * 1024 * 1024),
        name="finish",
    )(codes, smooth, master, one, two, small, mine)


def shards(
    grads,
    small_grads,
    counts,
    step,
    master,
    moment_one,
    moment_two,
    average,
    small_master,
    small_one,
    small_two,
    small_average,
):
    new_master, new_one, new_two, small, mine, codes, smooth = communicate(
        counts,
        step,
        small_grads,
        small_master,
        small_one,
        small_two,
        small_average,
        grads.transpose(0, 2, 1),
        master,
        moment_one,
        moment_two,
        average,
    )
    (weights, averages, new_master, new_one, new_two, small_new, small_new_one, small_new_two, small_weights, small_averages) = finish(
        codes, smooth, new_master, new_one, new_two, small, mine
    )
    return (
        new_master,
        new_one,
        new_two,
        small_new,
        small_new_one,
        small_new_two,
        weights.T,
        small_weights,
        averages.T,
        small_averages,
    )


def solution(mesh):
    placed = (
        P("shard", None, "tensor"),
        P("shard", "tensor"),
        P("shard"),
        P(),
        P(("shard", "tensor"), None),
        P(("shard", "tensor"), None),
        P(("shard", "tensor"), None),
        P(("shard", "tensor"), None),
        P("tensor", "shard"),
        P("tensor", "shard"),
        P("tensor", "shard"),
        P("tensor", "shard"),
    )
    return jax.shard_map(
        shards,
        mesh=mesh,
        in_specs=placed,
        out_specs=(
            P(("shard", "tensor"), None),
            P(("shard", "tensor"), None),
            P(("shard", "tensor"), None),
            P("tensor", "shard"),
            P("tensor", "shard"),
            P("tensor", "shard"),
            P(None, "tensor"),
            P("tensor"),
            P(None, "tensor"),
            P("tensor"),
        ),
        check_vma=False,
    )
```

```python
import jax
import jax.numpy as jnp
import numpy as np
from jax import lax
from jax.experimental import pallas as pl
from jax.experimental.pallas import tpu as pltpu
from jax.sharding import PartitionSpec as P

learn_rate = 0.002
beta_one = 0.9
beta_two = 0.999
adam_eps = 1e-08
weight_decay = 0.1
clip_norm = 1.0
decay_rate = 0.99

MESH = pl.DeviceIdType.MESH
RING = 4
SHARDS = RING * RING
TENSORS = 8
ROWS = 56
MINE = 7
COLS = 2080
ALL_COLS = COLS * TENSORS
SMALL = 368
SEG = 23
LANES = 384
PARTS = ((0, 512), (1536, 544), (512, 512), (1024, 512))
TOP = 32700.0
SUM_MAX = 2.0
AVERAGE_MAX = 0.02
WEIGHT_UNIT = 2.0**-33


def encode(x, most):
    scaled = jnp.abs(x) * (TOP**4 / most) + 1e-20
    root = (lax.rsqrt(lax.rsqrt(scaled)) + 0.5).astype(jnp.int32)
    return jnp.where(x < 0.0, -root, root).astype(jnp.int16)


def decode(code, most):
    root = code.astype(jnp.int32).astype(jnp.float32)
    return (root * root) * (root * jnp.abs(root)) * (most / TOP**4)


def encode_weight(x):
    units = jnp.minimum(jnp.abs(x) * (1.0 / WEIGHT_UNIT), 2147483520.0)
    whole = units.astype(jnp.int32)
    shift = jnp.zeros_like(whole)
    for bits in (16, 8, 4, 2, 1):
        shift = shift + jnp.where((whole >> shift) >= (1 << (bits + 10)), bits, 0)
    kept = whole >> shift
    cut = jnp.logical_or((kept << shift) != whole, whole.astype(jnp.float32) != units)
    code = ((shift << 10) + kept) | jnp.where(cut, 1, 0)
    return jnp.where(x < 0.0, -code, code).astype(jnp.int16)


def decode_weight(code):
    code = code.astype(jnp.int32)
    size = jnp.abs(code)
    shift = jnp.maximum((size >> 10) - 1, 0)
    value = ((size - (shift << 10)) << shift).astype(jnp.float32)
    return jnp.where(code < 0, -WEIGHT_UNIT, WEIGHT_UNIT) * value


def adam(param, first, second, gradient, bias_one, bias_two, decay):
    first_new = beta_one * first + (1.0 - beta_one) * gradient
    second_new = beta_two * second + (1.0 - beta_two) * gradient * gradient
    ratio = first_new / bias_one / (jnp.sqrt(second_new / bias_two) + adam_eps)
    return param - learn_rate * (ratio + decay * param), first_new, second_new


def bias(time, beta):
    total = jnp.float32(0.0)
    for bit in range(10):
        term = ((time >> bit) & 1).astype(jnp.float32) * (1.0 - float(np.float32(beta)) ** (1 << bit))
        total = total + term - total * term
    return total


def place(s, shape, along):
    own = lax.broadcasted_iota(jnp.int32, shape, along)
    every = lax.broadcasted_iota(jnp.int32, shape, 1 - along)
    return jnp.where(jnp.logical_and(every == own + SEG * s, own < SEG), 1.0, 0.0)


def exact_dot(a, b):
    return jnp.dot(a, b, precision=lax.Precision.HIGHEST, preferred_element_type=jnp.float32)


def wrap(position, shift, size):
    return lax.rem(position + (shift + size), size)


def step_kernel(
    counts,
    step,
    small_grads,
    small_master,
    small_one,
    small_two,
    small_average,
    grads_hbm,
    master_hbm,
    one_hbm,
    two_hbm,
    average_hbm,
    om,
    o1,
    o2,
    small_out,
    mine_out,
    wall,
    smooth_out,
    gv,
    loc,
    pm,
    p1,
    p2,
    pa,
    big_send,
    big_recv,
    kept,
    mid_send,
    mid_recv,
    total,
    chunk_send,
    chunk_recv,
    wchunk_send,
    wchunk_recv,
    achunk_send,
    achunk_recv,
    aall,
    norm_send,
    norm_t,
    norm_s,
    small_state,
    small_in,
    small_send,
    small_y,
    small_z,
    load_sem,
    rs_send_sem,
    rs_recv_sem,
    t_send_sem,
    t_recv_sem,
    n_send_sem,
    n_recv_sem,
    r_send_sem,
    r_recv_sem,
    ag_send_sem,
    ag_recv_sem,
):
    s = lax.axis_index("shard")
    t = lax.axis_index("tensor")
    pos = (lax.div(s, RING), lax.rem(s, RING))
    core_sign = 1 - 2 * lax.rem(t, 2)

    def ring_device(axis, p):
        return (p * RING + pos[1], t) if axis == 0 else (pos[0] * RING + p, t)

    def shard_of(axis, p, k):
        return p * RING + k if axis == 0 else k * RING + p

    barrier = pltpu.get_barrier_semaphore()
    for d in range(1, SHARDS):
        pl.semaphore_signal(barrier, inc=1, device_id=(wrap(s, d, SHARDS), t), device_id_type=MESH)
    for d in range(1, TENSORS):
        pl.semaphore_signal(barrier, inc=1, device_id=(s, wrap(t, d, TENSORS)), device_id_type=MESH)

    loads = [(average_hbm, pa)]
    for first, width in PARTS:
        cut = (slice(None), pl.ds(first, width))
        loads.append((grads_hbm.at[cut], gv.at[cut]))
    loads += [(master_hbm, pm), (one_hbm, p1), (two_hbm, p2)]
    loads = [pltpu.make_async_copy(src, dst, load_sem.at[i]) for i, (src, dst) in enumerate(loads)]
    for load in loads:
        load.start()

    valid_one = jnp.minimum(jnp.maximum(counts[0], 0), 1).astype(jnp.float32)
    valid_two = jnp.minimum(jnp.maximum(counts[0] - 1, 0), 1).astype(jnp.float32)
    small_state[...] = jnp.zeros((8, 128), jnp.float32)
    for i, ref in enumerate((small_master, small_one, small_two, small_average)):
        small_state[pl.ds(i + 1, 1), pl.ds(0, SEG)] = ref[...]
    small_in[...] = exact_dot(small_state[...], place(s, (128, LANES), 0))
    micro = small_grads[...].astype(jnp.float32)
    small_in[0:1, pl.ds(0, SMALL)] = valid_one * micro[0:1] + valid_two * micro[1:2]

    pending = []

    def send(src, dst, send_sem, recv_sem, device):
        copy = pltpu.make_async_remote_copy(
            src_ref=src, dst_ref=dst, send_sem=send_sem, recv_sem=recv_sem, device_id=device, device_id_type=MESH
        )
        copy.start()
        pending.append(copy)
        return copy

    def ring_share(kind, axis, src, dst):
        return [
            send(
                src,
                dst.at[d - 1],
                r_send_sem.at[kind, d - 1],
                r_recv_sem.at[kind, d - 1],
                ring_device(axis, wrap(pos[axis], d, RING)),
            )
            for d in range(1, RING)
        ]

    def exchange(kind, src, dst):
        copies = []
        for d in range(1, TENSORS):
            to = wrap(t, d, TENSORS)
            copies.append(
                send(src.at[to], dst.at[t], t_send_sem.at[kind, d], t_recv_sem.at[kind, d], (s, to))
            )
        return copies

    loads[0].wait()
    half = ALL_COLS // 2
    for h in range(2):
        codes = pa[:, pl.ds(half * h, half)]
        for j in range(4):
            achunk_send[4 * h + j] = encode(codes[:, COLS * j : COLS * (j + 1)], AVERAGE_MAX)
    achunk_recv[t] = achunk_send[t]


    def turn(q, tile):
        first, width = PARTS[q]
        cut = pl.ds(pl.multiple_of(tile * 128, 128), 128)
        a = gv[0, pl.ds(first, width), cut].astype(jnp.float32)
        b = gv[1, pl.ds(first, width), cut].astype(jnp.float32)
        loc[q][cut, :] = (valid_one * a + valid_two * b).T

    def local(shard, q):
        return loc[q][pl.ds(pl.multiple_of(shard * ROWS, 8), ROWS), :]

    axes = ((0, 1), (0, 1), (1, 0), (1, 0))
    signs = (core_sign, -core_sign, core_sign, -core_sign)
    order = [[wrap(pos[axes[q][1]], k, RING) for k in (2, signs[q], -signs[q], 0)] for q in range(4)]
    arrays = (wall, aall)

    def gather_send(x, q, shard, index, axis, sign):
        first, width = PARTS[q]
        ref = arrays[x].at[shard, :, pl.ds(first, width)]
        send(
            ref,
            ref,
            ag_send_sem.at[x, q, index],
            ag_recv_sem.at[x, q, index],
            ring_device(axis, wrap(pos[axis], sign, RING)),
        )

    def gather_wait(x, q, shard, index):
        first, width = PARTS[q]
        ref = arrays[x].at[shard, :, pl.ds(first, width)]
        pltpu.make_async_remote_copy(
            src_ref=ref,
            dst_ref=ref,
            send_sem=ag_send_sem.at[x, q, index],
            recv_sem=ag_recv_sem.at[x, q, index],
            device_id=ring_device(0, wrap(pos[0], 1, RING)),
            device_id_type=MESH,
        ).wait_recv()

    def outer(x, q, j, shard):
        axis, sign = axes[q][0], signs[q]
        gather_send(x, q, shard, 3 + 3 * j, axis, sign)
        gather_send(x, q, shard, 4 + 3 * j, axis, -sign)

    def source(q, shift, shift_outer):
        axis, other = axes[q]
        return shard_of(axis, wrap(pos[axis], shift_outer, RING), wrap(pos[other], shift, RING))

    def relay(x, q, j, shift):
        axis, sign = axes[q][0], signs[q]
        shard = source(q, shift, -sign)
        gather_wait(x, q, shard, 3 + 3 * j)
        gather_send(x, q, shard, 5 + 3 * j, axis, sign)

    def gather_first(x, q):
        other, sign = axes[q][1], signs[q]
        gather_send(x, q, s, 0, other, sign)
        gather_send(x, q, s, 1, other, -sign)
        outer(x, q, 0, s)

    def gather_second(x, q):
        other, sign = axes[q][1], signs[q]
        shard = source(q, -sign, 0)
        gather_wait(x, q, shard, 0)
        gather_send(x, q, shard, 2, other, sign)
        outer(x, q, 1, shard)
        relay(x, q, 0, 0)
        shard = source(q, sign, 0)
        gather_wait(x, q, shard, 1)
        outer(x, q, 2, shard)

    def gather_third(x, q):
        relay(x, q, 1, -signs[q])

    def gather_fourth(x, q):
        sign = signs[q]
        shard = source(q, 2, 0)
        gather_wait(x, q, shard, 2)
        outer(x, q, 3, shard)
        relay(x, q, 2, sign)

    def gather_fifth(x, q):
        relay(x, q, 3, 2)

    def gather_end(x, q):
        sign = signs[q]
        for j, shift in enumerate((0, -sign, sign, 2)):
            gather_wait(x, q, source(q, shift, sign), 4 + 3 * j)
            gather_wait(x, q, source(q, shift, 2), 5 + 3 * j)

    def turn_average(q):
        first, width = PARTS[q]
        for c in range(0, width, 128):
            some = min(128, width - c)
            codes = aall[:, :, pl.ds(first + c, some)].astype(jnp.int32).reshape(SHARDS * ROWS, some)
            smooth_out[pl.ds(first + c, some), :] = decay_rate * decode(codes.T, AVERAGE_MAX)

    early = [[None] * 2 for _ in range(4)]
    far = lax.min(lax.div(7 * wrap(pos[0], 2, RING), 4), 4)
    for slot in range(2):
        for q in (0, 2, 1, 3):
            axis, sign = axes[q][0], signs[q]
            p = pos[axis]
            dest = wrap(p, 2, RING) if slot == 0 else wrap(p, sign, RING)
            if slot == 0:
                loads[q + 1].wait()
            some = (0, 7) if axis == 1 else (0, 3) if slot == 0 else (3, 7)

            def tile(j, carry, q=q, axis=axis):
                turn(q, wrap(far, j, 7) if axis == 0 else j)
                return carry

            if slot == 0 or axis == 0:
                lax.fori_loop(*some, tile, 0)

            def fill(k, carry, q=q, axis=axis, dest=dest, slot=slot):
                big_send[q][slot, k] = encode(local(shard_of(axis, dest, k), q), SUM_MAX)
                return carry

            lax.fori_loop(0, RING, fill, 0)
            if slot == 0 and q == 0:
                pl.semaphore_wait(barrier, SHARDS - 1 + TENSORS - 1)
            to = wrap(p, -sign, RING) if slot == 0 else dest
            early[q][slot] = send(
                big_send[q].at[slot],
                big_recv[q].at[slot],
                rs_send_sem.at[q, slot],
                rs_recv_sem.at[q, slot],
                ring_device(axis, to),
            )
            if slot == 0 and q == 2:
                achunk_copies = exchange(3, achunk_send, achunk_recv)
                small_copies = ring_share(0, 0, small_in, small_y)
    relayed = [[None] * RING for _ in range(4)]
    for q in range(4):
        early[q][0].wait_recv()
    for i in range(RING):
        for q in range(4):
            axis, sign = axes[q][0], signs[q]
            dest = wrap(pos[axis], -sign, RING)
            k = order[q][i]
            came = decode(big_recv[q][0, k], SUM_MAX)
            big_send[q][2, k] = encode(local(shard_of(axis, dest, k), q) + came, 2 * SUM_MAX)
            relayed[q][i] = send(
                big_send[q].at[2, k],
                big_recv[q].at[2, k],
                rs_send_sem.at[q, 2 + i],
                rs_recv_sem.at[q, 2 + i],
                ring_device(axis, dest),
            )
    for copy in small_copies:
        copy.wait_recv()
    small_send[...] = small_in[...] + small_y[0] + small_y[1] + small_y[2]
    small_copies = ring_share(1, 1, small_send, small_z)
    for q in range(4):
        early[q][1].wait_recv()
    for copy in achunk_copies:
        copy.wait_recv()
    aall[s] = jnp.concatenate([achunk_recv[j].astype(jnp.int32) for j in range(TENSORS)], axis=0).astype(jnp.int16)

    later = [[None] * 3 for _ in range(4)]
    for i in range(RING):
        for q in range(4):
            (axis, other), sign = axes[q], signs[q]
            k = order[q][i]
            relayed[q][i].wait_recv()
            piece = (
                local(shard_of(axis, pos[axis], k), q)
                + decode(big_recv[q][1, k], SUM_MAX)
                + decode(big_recv[q][2, k], 2 * SUM_MAX)
            )
            if i >= 2:
                kept[q][i - 2] = piece
                continue
            mid_send[q][i] = encode(piece, 4 * SUM_MAX)
            to = wrap(pos[other], -sign if i == 0 else sign, RING)
            later[q][i] = send(
                mid_send[q].at[i],
                mid_recv[q].at[i],
                rs_send_sem.at[q, 6 + i],
                rs_recv_sem.at[q, 6 + i],
                ring_device(other, to),
            )
    for q in range(4):
        other, sign = axes[q][1], signs[q]
        later[q][0].wait_recv()
        mid_send[q][2] = encode(kept[q][0] + decode(mid_recv[q][0], 4 * SUM_MAX), 8 * SUM_MAX)
        later[q][2] = send(
            mid_send[q].at[2],
            mid_recv[q].at[2],
            rs_send_sem.at[q, 8],
            rs_recv_sem.at[q, 8],
            ring_device(other, wrap(pos[other], -sign, RING)),
        )
    for q in range(4):
        gather_first(1, q)
    for copy in small_copies:
        copy.wait_recv()
    small_all = small_send[...] + small_z[0] + small_z[1] + small_z[2]
    small_sum = small_all[0:1]
    squares = jnp.sum(small_sum * small_sum) * (1.0 / SHARDS)
    for q in range(4):
        first, width = PARTS[q]
        later[q][1].wait_recv()
        later[q][2].wait_recv()
        piece = kept[q][1] + decode(mid_recv[q][1], 4 * SUM_MAX) + decode(mid_recv[q][2], 8 * SUM_MAX)
        total[:, pl.ds(first, width)] = piece
        squares = squares + jnp.sum(piece * piece)

    norm_send[0] = jnp.full((8, 128), squares, jnp.float32)
    norm_copies = []
    for d in range(1, TENSORS):
        norm_copies.append(
            send(
                norm_send.at[0],
                norm_t.at[d - 1],
                t_send_sem.at[0, d],
                t_recv_sem.at[0, d],
                (s, wrap(t, d, TENSORS)),
            )
        )
    for j in range(TENSORS):
        chunk_send[j] = encode(total[pl.ds(MINE * j, MINE), :], 16 * SUM_MAX)
    chunk_recv[t] = chunk_send[t]

    chunk_copies = exchange(1, chunk_send, chunk_recv)
    for copy in norm_copies:
        copy.wait_recv()
    norm = norm_send[0]
    for d in range(TENSORS - 1):
        norm = norm + norm_t[d]
    norm_send[1] = norm
    norm_copies = []
    for d in range(1, SHARDS):
        to = wrap(s, d, SHARDS)
        norm_copies.append(
            send(norm_send.at[1], norm_s.at[s], n_send_sem.at[d], n_recv_sem.at[d], (to, t))
        )
    norm_s[s] = norm
    for q in range(4):
        gather_second(1, q)
    for copy in norm_copies:
        copy.wait_recv()
    norm = norm_s[0]
    for d in range(1, SHARDS):
        norm = norm + norm_s[d]
    norm = jnp.sqrt(norm)
    factor = jnp.minimum(1.0, clip_norm / (norm + 1e-06))[0:1, 0:1]

    bias_one, bias_two = bias(step[0], beta_one), bias(step[0], beta_two)
    for load in loads[5:]:
        load.wait()
    for copy in chunk_copies:
        copy.wait_recv()
    for q in range(4):
        gather_third(1, q)
    for h in range(2):
        cols = pl.ds(half * h, half)
        summed = jnp.concatenate([decode(chunk_recv[4 * h + j], 16 * SUM_MAX) for j in range(4)], axis=1)
        new, one, two = adam(pm[:, cols], p1[:, cols], p2[:, cols], summed * factor, bias_one, bias_two, weight_decay)
        om[:, cols] = new
        o1[:, cols] = one
        o2[:, cols] = two
        for j in range(4):
            wchunk_send[4 * h + j] = encode_weight(new[:, COLS * j : COLS * (j + 1)])
    wchunk_recv[t] = wchunk_send[t]
    wchunk_copies = exchange(2, wchunk_send, wchunk_recv)

    new, one, two = adam(
        small_all[1:2], small_all[2:3], small_all[3:4], small_sum * factor, bias_one, bias_two, 0.0
    )
    smooth = decay_rate * small_all[4:5] + (1.0 - decay_rate) * new
    small_out[0:1] = new
    small_out[1:2] = one
    small_out[2:3] = two
    small_out[3:4] = smooth
    small_out[4:8] = jnp.zeros((4, LANES), jnp.float32)
    mine_out[...] = exact_dot(small_out[...], place(s, (LANES, 128), 1))

    for q in range(4):
        gather_fourth(1, q)
    for copy in wchunk_copies:
        copy.wait_recv()
    wall[s] = jnp.concatenate([wchunk_recv[j].astype(jnp.int32) for j in range(TENSORS)], axis=0).astype(jnp.int16)
    for q in range(4):
        gather_first(0, q)
    for q in range(4):
        gather_fifth(1, q)
    for q in range(4):
        gather_second(0, q)
    for q in range(4):
        gather_end(1, q)
    for q in range(4):
        gather_third(0, q)
    for q in range(4):
        gather_fourth(0, q)
    for q in range(4):
        gather_fifth(0, q)
    for i in range(4):
        turn_average(i)
    for q in range(4):
        gather_end(0, q)
    for copy in pending:
        copy.wait_send()


def communicate(*args):
    hbm = pl.BlockSpec(memory_space=pl.ANY)
    vmem = pl.BlockSpec(memory_space=pltpu.VMEM)
    smem = pl.BlockSpec(memory_space=pltpu.SMEM)
    f32, bf16, i16 = jnp.float32, jnp.bfloat16, jnp.int16
    widths = [w for _, w in PARTS]
    chunk = (TENSORS, MINE, COLS)
    return pl.pallas_call(
        step_kernel,
        out_shape=(
            *[pltpu.VMEM((MINE, ALL_COLS), f32)] * 3,
            pltpu.VMEM((8, LANES), f32),
            pltpu.VMEM((8, 128), f32),
            pltpu.VMEM((SHARDS, ROWS, COLS), i16),
            pltpu.VMEM((COLS, SHARDS * ROWS), f32),
        ),
        in_specs=[smem] * 2 + [vmem] * 5 + [hbm] * 5,
        out_specs=(vmem,) * 7,
        scratch_shapes=[
            pltpu.VMEM((2, COLS, SHARDS * ROWS), bf16),
            [pltpu.VMEM((SHARDS * ROWS, w), f32) for w in widths],
            *[pltpu.VMEM((MINE, ALL_COLS), f32)] * 4,
            [pltpu.VMEM((3, RING, ROWS, w), i16) for w in widths],
            [pltpu.VMEM((3, RING, ROWS, w), i16) for w in widths],
            [pltpu.VMEM((2, ROWS, w), f32) for w in widths],
            [pltpu.VMEM((3, ROWS, w), i16) for w in widths],
            [pltpu.VMEM((3, ROWS, w), i16) for w in widths],
            pltpu.VMEM((ROWS, COLS), f32),
            pltpu.VMEM(chunk, i16),
            pltpu.VMEM(chunk, i16),
            pltpu.VMEM(chunk, i16),
            pltpu.VMEM(chunk, i16),
            pltpu.VMEM(chunk, i16),
            pltpu.VMEM(chunk, i16),
            pltpu.VMEM((SHARDS, ROWS, COLS), i16),
            pltpu.VMEM((2, 8, 128), f32),
            pltpu.VMEM((TENSORS - 1, 8, 128), f32),
            pltpu.VMEM((SHARDS, 8, 128), f32),
            pltpu.VMEM((8, 128), f32),
            pltpu.VMEM((8, LANES), f32),
            pltpu.VMEM((8, LANES), f32),
            pltpu.VMEM((RING - 1, 8, LANES), f32),
            pltpu.VMEM((RING - 1, 8, LANES), f32),
            pltpu.SemaphoreType.DMA((8,)),
            pltpu.SemaphoreType.DMA((4, 9)),
            pltpu.SemaphoreType.DMA((4, 9)),
            pltpu.SemaphoreType.DMA((4, TENSORS)),
            pltpu.SemaphoreType.DMA((4, TENSORS)),
            pltpu.SemaphoreType.DMA((SHARDS,)),
            pltpu.SemaphoreType.DMA((SHARDS,)),
            pltpu.SemaphoreType.DMA((2, RING - 1)),
            pltpu.SemaphoreType.DMA((2, RING - 1)),
            pltpu.SemaphoreType.DMA((2, 4, 15)),
            pltpu.SemaphoreType.DMA((2, 4, 15)),
        ],
        compiler_params=pltpu.CompilerParams(
            collective_id=0, has_side_effects=True, vmem_limit_bytes=48 * 1024 * 1024
        ),
        name="step",
    )(*args)


TURN = 512


def finish_kernel(
    codes,
    smooth,
    master,
    one,
    two,
    small,
    mine,
    weights_out,
    average_out,
    master_out,
    one_out,
    two_out,
    small_out,
    small_one_out,
    small_two_out,
    small_weights_out,
    small_average_out,
):
    step = pl.program_id(0)
    last = COLS // TURN

    def turn(width, first):
        cut = (slice(None), slice(None), pl.ds(first, width))
        new = decode_weight(codes[cut].astype(jnp.int32).reshape(SHARDS * ROWS, width).T)
        weights_out[pl.ds(0, width), :] = new.astype(jnp.bfloat16)
        average_out[pl.ds(0, width), :] = smooth[pl.ds(first, width), :] + (1.0 - decay_rate) * new

    @pl.when(step < last)
    def _():
        turn(TURN, pl.multiple_of(step * TURN, TURN))

    @pl.when(step == last)
    def _():
        turn(COLS - last * TURN, last * TURN)

    @pl.when(step == 0)
    def _():
        master_out[...] = master[...]
        one_out[...] = one[...]
        two_out[...] = two[...]
        small_out[...] = mine[0:1, 0:SEG]
        small_one_out[...] = mine[1:2, 0:SEG]
        small_two_out[...] = mine[2:3, 0:SEG]
        small_weights_out[...] = small[0, 0:SMALL].astype(jnp.bfloat16)
        small_average_out[...] = small[3, 0:SMALL]


def finish(codes, smooth, master, one, two, small, mine):
    def whole(*shape):
        return pl.BlockSpec(shape, lambda i: (0,) * len(shape))

    vmem = pl.BlockSpec(memory_space=pltpu.VMEM)
    f32, bf16 = jnp.float32, jnp.bfloat16
    rows = jax.ShapeDtypeStruct((MINE, ALL_COLS), f32)
    few = jax.ShapeDtypeStruct((1, SEG), f32)
    turned = pl.BlockSpec((TURN, SHARDS * ROWS), lambda i: (i, 0))
    return pl.pallas_call(
        finish_kernel,
        grid=(pl.cdiv(COLS, TURN),),
        in_specs=[vmem] * 7,
        out_specs=[turned, turned] + [whole(MINE, ALL_COLS)] * 3 + [whole(1, SEG)] * 3 + [whole(SMALL)] * 2,
        out_shape=(
            jax.ShapeDtypeStruct((COLS, SHARDS * ROWS), bf16),
            jax.ShapeDtypeStruct((COLS, SHARDS * ROWS), f32),
            rows,
            rows,
            rows,
            few,
            few,
            few,
            jax.ShapeDtypeStruct((SMALL,), bf16),
            jax.ShapeDtypeStruct((SMALL,), f32),
        ),
        compiler_params=pltpu.CompilerParams(vmem_limit_bytes=32 * 1024 * 1024),
        name="finish",
    )(codes, smooth, master, one, two, small, mine)


def shards(
    grads,
    small_grads,
    counts,
    step,
    master,
    moment_one,
    moment_two,
    average,
    small_master,
    small_one,
    small_two,
    small_average,
):
    new_master, new_one, new_two, small, mine, codes, smooth = communicate(
        counts,
        step,
        small_grads,
        small_master,
        small_one,
        small_two,
        small_average,
        grads.transpose(0, 2, 1),
        master,
        moment_one,
        moment_two,
        average,
    )
    (weights, averages, new_master, new_one, new_two, small_new, small_new_one, small_new_two, small_weights, small_averages) = finish(
        codes, smooth, new_master, new_one, new_two, small, mine
    )
    return (
        new_master,
        new_one,
        new_two,
        small_new,
        small_new_one,
        small_new_two,
        weights.T,
        small_weights,
        averages.T,
        small_averages,
    )


def solution(mesh):
    placed = (
        P("shard", None, "tensor"),
        P("shard", "tensor"),
        P("shard"),
        P(),
        P(("shard", "tensor"), None),
        P(("shard", "tensor"), None),
        P(("shard", "tensor"), None),
        P(("shard", "tensor"), None),
        P("tensor", "shard"),
        P("tensor", "shard"),
        P("tensor", "shard"),
        P("tensor", "shard"),
    )
    return jax.shard_map(
        shards,
        mesh=mesh,
        in_specs=placed,
        out_specs=(
            P(("shard", "tensor"), None),
            P(("shard", "tensor"), None),
            P(("shard", "tensor"), None),
            P("tensor", "shard"),
            P("tensor", "shard"),
            P("tensor", "shard"),
            P(None, "tensor"),
            P("tensor"),
            P(None, "tensor"),
            P("tensor"),
        ),
        check_vma=False,
    )
```
